32 devices in a mesh: groups: 2 (over y), arow: 16 (over z, x, core).
Axes of the slice: x: 2, y: 2, z: 4, core: 2. Of those that a mesh axis runs over, the one named last changes fastest.
Arguments:
- feat_a: bfloat16 [64, 32, 256], P(('groups', 'arow')), parts along dimension 0, may hold values from -6 to 6
- feat_b: bfloat16 [32, 32, 256], P(('groups', 'arow')), parts along dimension 0, may hold values from -6 to 6
- a_first: float32 [8, 3, 3], replicated, may hold values from -2 to 2
- b_first: float32 [8, 3, 3], replicated, may hold values from -2 to 2
- bias_first: float32 [8], replicated, may hold values from -3 to 3
- a_second: float32 [8, 3, 3], replicated, may hold values from -1.5 to 1.5
- b_second: float32 [8, 3, 3], replicated, may hold values from -1.5 to 1.5
- bias_second: float32 [1], replicated, may hold values from -3 to 3
Outputs:
- matches: float32 [64, 32, 512], P(('groups', 'arow')), parts along dimension 0
The draws below stay inside these ranges and needn't reach their ends.
There are 2 independent parts, one for each index of `groups`. The reference program is written for one: setup_inputs(seed, part) draws one part's arguments, and reference() takes and returns one part's arrays. A program takes and returns all parts, laid end to end along the dimension named above; an argument that names none is the same for every part. Nothing has to cross between parts.
All inputs are finite; a program needn't handle non-finite values.
Results may differ from the reference program's by a relative error of at most 0.0081.
Values may be sent and summed in bfloat16 or wider, within the bound.
No kernel may reach another device: no remote copies, remote signals or barrier semaphores. Data moves between devices by JAX's collectives and lax.ppermute only.
A program may use at most 128 MiB of HBM per device.

```python
import jax
import jax.numpy as jnp
from jax import lax

C = 256
HID = 8
W = 32
HA = 32
HB = 16


def block_levels(own_key, shape, pieces, low, high):
    level = 1.0
    for position, blocks in pieces:
        heights = jax.random.uniform(jax.random.fold_in(jax.random.fold_in(own_key, 6), position), (blocks,), jnp.float32, low / len(pieces), high / len(pieces))
        level = level * jnp.repeat(jnp.exp(heights), shape[position] // blocks).reshape((-1,) + (1,) * (len(shape) - 1 - position))
    return level


def normal_values(stream_key, dims, scale, reach, pieces=(), held_as=jnp.bfloat16):
    factor_of = block_levels(stream_key, dims, pieces, -0.22, 0.18) if pieces else 1.0
    drawn = jax.random.normal(stream_key, dims, jnp.float32) * scale * factor_of
    return jnp.minimum(jnp.maximum(drawn, -reach), reach).astype(held_as)


def setup_inputs(seed: int = 0, part: int = 0) -> dict:
    streams_of = jax.random.split(jax.random.key(seed), 9)
    part_splits = jax.random.split(jax.random.fold_in(streams_of[8], part), 9)
    feat_a = normal_values(part_splits[0], (HA, W, C), 1.0, 6.0, ((0, 16),))
    feat_b = normal_values(part_splits[1], (HB, W, C), 1.0, 6.0, ((0, 16),))
    a_first = normal_values(streams_of[2], (HID, 3, 3), 0.33, 2.0, (), jnp.float32)
    b_first = normal_values(streams_of[3], (HID, 3, 3), 0.33, 2.0, (), jnp.float32)
    bias_first = normal_values(streams_of[4], (HID,), 0.5, 3.0, (), jnp.float32)
    a_second = normal_values(streams_of[5], (HID, 3, 3), 0.25, 1.5, (), jnp.float32)
    b_second = normal_values(streams_of[6], (HID, 3, 3), 0.25, 1.5, (), jnp.float32)
    bias_second = normal_values(streams_of[7], (1,), 0.5, 3.0, (), jnp.float32)
    return {"feat_a": feat_a, "feat_b": feat_b, "a_first": a_first, "b_first": b_first, "bias_first": bias_first, "a_second": a_second, "b_second": b_second, "bias_second": bias_second}


EPSILON = 1e-5


def shifted_zero(values, along, offset):
    extent = values.shape[along]
    if offset == 0:
        return values
    widths = [(0, 0)] * values.ndim
    if offset > 0:
        widths[along] = (0, offset)
        return lax.slice_in_dim(jnp.pad(values, widths), offset, offset + extent, axis=along)
    widths[along] = (-offset, 0)
    return lax.slice_in_dim(jnp.pad(values, widths), 0, extent, axis=along)


def conv_a(values, kernel):
    out_rows = values.shape[-3] - 2
    result = 0.0
    for row_tap in range(3):
        row_slab = lax.slice_in_dim(values, row_tap, row_tap + out_rows, axis=values.ndim - 3).astype(jnp.float32)
        for col_tap in range(3):
            result = result + kernel[..., row_tap, col_tap][..., None, None, None] * shifted_zero(row_slab, values.ndim - 2, col_tap - 1)
    return result


def conv_b(values, kernel, map_width):
    flat_pos = lax.broadcasted_iota(jnp.int32, (values.shape[-1],), 0) % map_width
    result = 0.0
    for row_tap in range(3):
        for col_tap in range(3):
            shifted = shifted_zero(values, values.ndim - 1, (row_tap - 1) * map_width + (col_tap - 1))
            inside = ((flat_pos + col_tap - 1 >= 0) & (flat_pos + col_tap - 1 < map_width)).astype(jnp.float32)
            result = result + kernel[..., row_tap, col_tap][..., None, None, None] * (shifted * inside)
    return result


def consensus(correlation, kern_a1, kern_b1, bias_one, kern_a2, kern_b2, bias_two, map_width):
    padded = jnp.pad(correlation, ((1, 1), (0, 0), (0, 0)))

    def one_channel(running, members):
        first_a, first_b, bias_value, second_a, second_b = members
        hidden = jax.nn.relu(conv_b(conv_a(padded, first_a), first_b, map_width) + bias_value).astype(jnp.bfloat16)
        hidden_pad = jnp.pad(hidden, ((1, 1), (0, 0), (0, 0)))
        return running + conv_b(conv_a(hidden_pad, second_a), second_b, map_width), None

    running, unused = lax.scan(one_channel, jnp.zeros(correlation.shape, jnp.float32), (kern_a1, kern_b1, bias_one, kern_a2, kern_b2))
    return jax.nn.relu(running + bias_two[0])


def reference(feat_a, feat_b, a_first, b_first, bias_first, a_second, b_second, bias_second):
    product = jnp.dot(feat_a.reshape(HA * W, C), feat_b.reshape(HB * W, C).T, preferred_element_type=jnp.float32)
    correlation = (product * (C ** -0.5)).astype(jnp.bfloat16).reshape(HA, W, HB * W)
    score = consensus(correlation, a_first, b_first, bias_first, a_second, b_second, bias_second, W)
    score = score + consensus(correlation, b_first, a_first, bias_first, b_second, a_second, bias_second, W)
    best_over_a = jnp.max(score, axis=(0, 1))
    best_over_b = jnp.max(score, axis=2)[..., None]
    return score * (score / (best_over_a + EPSILON)) * (score / (best_over_b + EPSILON))
```

```python
import functools

import jax
import jax.numpy as jnp
from jax import lax
from jax.experimental import pallas as pl
from jax.experimental.pallas import tpu as pltpu
from jax.sharding import PartitionSpec as P

EPSILON = 1e-05
F32 = jnp.float32
BF16 = jnp.bfloat16


def padded(cells, sides, width):
    for axis, dim in sides:
        count = lax.axis_size(axis)
        ends = count - 1
        head = lax.slice_in_dim(cells, 0, width, axis=dim)
        tail = lax.slice_in_dim(cells, cells.shape[dim] - width, cells.shape[dim], axis=dim)
        cells = jnp.concatenate(
            [
                lax.ppermute(tail, axis, [(i, (i + 1) % count) for i in range(ends)]),
                cells,
                lax.ppermute(head, axis, [((i + 1) % count, i) for i in range(ends)]),
            ],
            axis=dim,
        )
    return cells


def shifted_zero(values, along, offset):
    extent = values.shape[along]
    if offset == 0:
        return values
    widths = [(0, 0)] * values.ndim
    if offset > 0:
        widths[along] = (0, offset)
        return lax.slice_in_dim(jnp.pad(values, widths), offset, offset + extent, axis=along)
    widths[along] = (-offset, 0)
    return lax.slice_in_dim(jnp.pad(values, widths), 0, extent, axis=along)


def conv_a(values, kernel):
    out_rows = values.shape[-3] - 2
    result = 0.0
    for row_tap in range(3):
        row_slab = lax.slice_in_dim(
            values, row_tap, row_tap + out_rows, axis=values.ndim - 3
        ).astype(F32)
        for col_tap in range(3):
            result = result + kernel[..., row_tap, col_tap][..., None, None, None] * shifted_zero(
                row_slab, values.ndim - 2, col_tap - 1
            )
    return result


def conv_b(values, kernel, map_width):
    flat_pos = lax.broadcasted_iota(jnp.int32, (values.shape[-1],), 0) % map_width
    result = 0.0
    for row_tap in range(3):
        for col_tap in range(3):
            shifted = shifted_zero(
                values, values.ndim - 1, (row_tap - 1) * map_width + (col_tap - 1)
            )
            inside = ((flat_pos + col_tap - 1 >= 0) & (flat_pos + col_tap - 1 < map_width)).astype(
                F32
            )
            result = result + kernel[..., row_tap, col_tap][..., None, None, None] * (
                shifted * inside
            )
    return result


def first_layer(correlation, kern_a, kern_b, bias_one, map_width):
    spread = conv_a(correlation, kern_a)
    return jax.nn.relu(conv_b(spread, kern_b, map_width) + bias_one[:, None, None, None]).astype(
        BF16
    )


def second_layer(hidden, kern_a, kern_b, bias_two, map_width):
    spread = conv_a(hidden, kern_a)
    summed = jnp.sum(conv_b(spread, kern_b, map_width), axis=0)
    return jax.nn.relu(summed + bias_two[0])


def general(feat_a, feat_b, a_first, b_first, bias_first, a_second, b_second, bias_second):
    map_width = feat_b.shape[1]
    channels = feat_a.shape[2]
    b_cells = feat_b.shape[0] * lax.axis_size("arow") * map_width
    a_rows = feat_a.reshape(-1, channels)
    tile_product = lax.dot_general(
        a_rows,
        lax.all_gather(feat_b, "arow", axis=0, tiled=True).reshape(-1, channels),
        (((1,), (1,)), ((), ())),
        preferred_element_type=F32,
    )
    correlation = (
        (tile_product * channels ** (-0.5))
        .astype(BF16)
        .reshape(feat_a.shape[0], map_width, b_cells)
    )
    correlation = padded(correlation, (("arow", 0),), 1)

    def network(kern_a1, kern_b1, kern_a2, kern_b2):
        hidden = first_layer(correlation, kern_a1, kern_b1, bias_first, map_width)
        hidden = padded(hidden, (("arow", 1),), 1)
        return second_layer(hidden, kern_a2, kern_b2, bias_second, map_width)

    score = network(a_first, b_first, a_second, b_second)
    score = score + network(b_first, a_first, b_second, a_second)
    best_over_a = lax.pmax(jnp.max(score, axis=(0, 1)), "arow")
    best_over_b = jnp.max(score, axis=2)[..., None]
    return score * (score / (best_over_a + EPSILON)) * (score / (best_over_b + EPSILON))


def lane(shape):
    return lax.broadcasted_iota(jnp.int32, shape, 1)


def sublane(shape):
    return lax.broadcasted_iota(jnp.int32, shape, 0)


def two_terms(value):
    high = value.astype(BF16)
    return high, (value - high.astype(F32)).astype(BF16)


def first_weights(taps, at_ref, k, width):
    col = lane((width, 128)) % width
    diag = [sublane((width, 128)) + 1 - col == w for w in range(3)]
    row = lane((1, 128)) // width
    for net in range(2):
        lanes = slice(128 * net, 128 * net + 128)
        for cr in range(6):
            block = jnp.zeros((width, 128), F32)
            for w in range(3):
                per_lane = jnp.zeros((1, 128), F32)
                for u in range(3):
                    if 0 <= cr - u <= 3:
                        per_lane = jnp.where(row == cr - u, taps[net][k * 9 + 3 * u + w], per_lane)
                block = jnp.where(diag[w], per_lane, block)
            high, low = two_terms(block)
            at_ref[k, cr * width : (cr + 1) * width, lanes] = high
            at_ref[k, (8 + cr) * width : (9 + cr) * width, lanes] = low
        for base in (6, 14):
            at_ref[k, base * width : (base + 2) * width, lanes] = jnp.zeros((2 * width, 128), BF16)


def second_weights(taps, at_ref, k, width, keep):
    col = lane((width, 128)) % width
    diag = [sublane((width, 128)) + 1 - col == w for w in range(3)]
    row = lane((1, 128)) // width
    for net in range(2):
        for hr in range(4):
            block = jnp.zeros((width, 128), F32)
            for w in range(3):
                per_lane = jnp.zeros((1, 128), F32)
                for u in range(3):
                    if 0 <= hr - u <= 1:
                        tap = taps[net][k * 9 + 3 * u + w]
                        if hr in keep:
                            tap = tap * keep[hr]
                        per_lane = jnp.where(row == 2 * net + hr - u, tap, per_lane)
                block = jnp.where(diag[w], per_lane, block)
            high, low = two_terms(block)
            rows = slice((4 * net + hr) * width, (4 * net + hr + 1) * width)
            at_ref[k, rows, 0:128] = high
            at_ref[k, rows, 128:256] = low


def b_taps(load, weights, emit, width):
    top = sublane((8, 128)) == 0
    bottom = sublane((8, 128)) == 7

    def column(jb):
        even, odd = load(2 * jb), load(2 * jb + 1)
        above = jnp.where(top, 0.0, pltpu.roll(odd, 1, 0))
        below = jnp.where(bottom, 0.0, pltpu.roll(even, 7, 0))
        return above, even, odd, below

    window = [None, column(0), column(1)]
    for jb in range(width):
        sums = []
        for par in range(2):
            total = None
            for t in range(3):
                if window[t] is None:
                    continue
                for s in range(3):
                    term = weights[3 * s + t] * window[t][par + s]
                    total = term if total is None else total + term
            sums.append(total)
        emit(jb, sums[0], sums[1])
        window = [window[1], window[2], column(jb + 2) if jb + 2 < width else None]


def consensus_kernel(
    offsets,
    width,
    info_ref,
    a1_ref,
    b1_ref,
    bias1_ref,
    a2_ref,
    b2_ref,
    bias2_ref,
    own_ref,
    mate_ref,
    outer_ref,
    score_ref,
    part_ref,
    best_ref,
    fa_ref,
    vf_ref,
    vp_ref,
    at1_ref,
    at2_ref,
    s_ref,
    h_ref,
    t_ref,
    acc_ref,
    nat_ref,
):
    half = len(offsets)
    channels = own_ref.shape[2]
    cells = 2 * half * width
    index = info_ref[0]
    parity = info_ref[1]
    keep_low = info_ref[2].astype(F32)
    keep_high = info_ref[3].astype(F32)
    first = (a1_ref, b1_ref)
    second = (a2_ref, b2_ref)

    for k in range(8):
        first_weights(first, at1_ref, k, width)
        second_weights(second, at2_ref, k, width, {0: keep_low, 3: keep_high})

    fa_ref[2:4] = own_ref[half : half + 2]
    fa_ref[pl.ds(4 - 4 * parity, 2)] = mate_ref[half : half + 2]
    keep_outer = (keep_low * keep_high).astype(BF16)
    fa_ref[pl.ds(4 * parity, 2)] = outer_ref[...] * keep_outer
    fa_ref[6:8] = jnp.zeros((2, width, channels), BF16)
    rows = fa_ref[...].reshape(8 * width, channels)

    for side, ref in enumerate((own_ref, mate_ref)):
        product = lax.dot_general(
            ref[0:half].reshape(half * width, channels),
            rows,
            (((1,), (1,)), ((), ())),
            preferred_element_type=F32,
        )
        for g in range(half):
            ib = index ^ (offsets[g] ^ side)
            start = (ib % 2) * 8 + ib // 2
            block = product[g * width : (g + 1) * width] * channels ** (-0.5)
            for c in range(2):
                vf_ref[c, pl.ds(start, width, stride=16), :] = block[
                    :, 128 * c : 128 * c + 128
                ]
    for c in range(4):
        vp_ref[:, 128 * c : 128 * c + 128] = vf_ref[c % 2].astype(BF16)

    half_lanes = lane((1, 128)) < 64
    for k in range(8):
        s_ref[k % 2] = jnp.dot(vp_ref[...], at1_ref[k], preferred_element_type=F32)
        for net in range(2):
            bank = first[1 - net]
            weights = [bank[k * 9 + tap] for tap in range(9)]
            bias = bias1_ref[k]

            def load(r, net=net, k=k):
                return s_ref[k % 2, 8 * r : 8 * r + 8, 128 * net : 128 * net + 128]

            def emit(jb, even, odd, net=net, k=k, bias=bias):
                pair = jnp.concatenate([even, odd], axis=0)
                h_ref[k % 2, 16 * jb : 16 * jb + 16, 128 * net : 128 * net + 128] = jnp.maximum(
                    pair + bias, 0.0
                ).astype(BF16)

            b_taps(load, weights, emit, width)
        both = jnp.dot(h_ref[k % 2], at2_ref[k], preferred_element_type=F32)
        t_ref[k % 2] = both[:, 0:128] + both[:, 128:256]
        weights = [
            jnp.where(half_lanes, second[1][k * 9 + tap], second[0][k * 9 + tap])
            for tap in range(9)
        ]

        def load(r, k=k):
            return t_ref[k % 2, 8 * r : 8 * r + 8, :]

        def emit(jb, even, odd, k=k):
            pair = jnp.concatenate([even, odd], axis=0)
            if k == 0:
                acc_ref[16 * jb : 16 * jb + 16, :] = pair
            elif k < 7:
                acc_ref[16 * jb : 16 * jb + 16, :] += pair
            else:
                total = jnp.maximum(
                    acc_ref[16 * jb : 16 * jb + 16, :] + pair + bias2_ref[0], 0.0
                )
                nat_ref[pl.ds(jb, 8, stride=2 * width), :] = total[0:8]
                nat_ref[pl.ds(width + jb, 8, stride=2 * width), :] = total[8:16]

        b_taps(load, weights, emit, width)

    turned = jnp.transpose(nat_ref[...], (1, 0))
    score = turned[0:64] + turned[64:128]
    best_ref[...] = jnp.max(score, axis=0, keepdims=True)
    best_b = jnp.max(score, axis=1, keepdims=True)
    score_ref[...] = score
    part_ref[...] = score * (score / (best_b + EPSILON))


def consensus(info, filters, own, mate, outer, offsets, width):
    half = len(offsets)
    cells = 2 * half * width
    channels = own.shape[2]
    smem = pl.BlockSpec(memory_space=pltpu.SMEM)
    vmem = pl.BlockSpec(memory_space=pltpu.VMEM)
    a1, b1, bias1, a2, b2, bias2 = filters
    return pl.pallas_call(
        functools.partial(consensus_kernel, offsets, width),
        out_shape=(
            jax.ShapeDtypeStruct((2 * width, cells), F32),
            jax.ShapeDtypeStruct((2 * width, cells), F32),
            jax.ShapeDtypeStruct((1, cells), F32),
        ),
        in_specs=[smem] * 7 + [vmem] * 3,
        out_specs=(vmem, vmem, vmem),
        scratch_shapes=[
            pltpu.VMEM((8, width, channels), BF16),
            pltpu.VMEM((2, cells, 128), F32),
            pltpu.VMEM((cells, 512), BF16),
            pltpu.VMEM((8, 512, 256), BF16),
            pltpu.VMEM((8, 256, 256), BF16),
            pltpu.VMEM((2, cells, 256), F32),
            pltpu.VMEM((2, cells, 256), BF16),
            pltpu.VMEM((2, cells, 128), F32),
            pltpu.VMEM((cells, 128), F32),
            pltpu.VMEM((cells, 128), F32),
        ],
        compiler_params=pltpu.CompilerParams(vmem_limit_bytes=32 << 20),
    )(
        info,
        a1.reshape(-1),
        b1.reshape(-1),
        bias1,
        a2.reshape(-1),
        b2.reshape(-1),
        bias2,
        own,
        mate,
        outer,
    )


def exchange(value, mask, count):
    return lax.ppermute(value, "arow", [(i, i ^ mask) for i in range(count)])


def outer_pairs(groups, count):
    pairs = []
    for g in range(groups):
        for i in range(count):
            j = i + 1 if i % 2 else i - 1
            if 0 <= j < count:
                pairs.append((g * count + i, g * count + j))
            else:
                other = g ^ 1 if (g ^ 1) < groups else g
                pairs.append((g * count + i, other * count + i))
    return pairs


def fast(feat_a, feat_b, a_first, b_first, bias_first, a_second, b_second, bias_second):
    count = lax.axis_size("arow")
    groups = lax.axis_size("groups")
    width = feat_b.shape[1]
    index = lax.axis_index("arow")
    masks = [(1 << b) | 1 for b in reversed(range(1, count.bit_length() - 1))]

    held, offsets = feat_b, [0]
    outer = None
    for n, mask in enumerate(masks):
        if n == 1:
            tied, held = lax.optimization_barrier((feat_a, held))
            outer = lax.ppermute(tied, ("groups", "arow"), outer_pairs(groups, count))
        held = jnp.concatenate([held, exchange(held, mask, count)], axis=0)
        offsets = offsets + [o ^ mask for o in offsets]
    own = jnp.concatenate([held, feat_a], axis=0)
    mate = exchange(own, 1, count)

    info = jnp.stack(
        [
            index,
            index % 2,
            (index != 0).astype(jnp.int32),
            (index != count - 1).astype(jnp.int32),
        ]
    ).astype(jnp.int32)
    filters = (a_first, b_first, bias_first, a_second, b_second, bias_second)
    score, part, best = consensus(info, filters, own, mate, outer, offsets, width)
    for mask in masks + [1]:
        best = jnp.maximum(best, exchange(best, mask, count))
    out = part * (score / (best + EPSILON))
    return out.reshape(feat_a.shape[0], width, -1)


def on_device(feat_a, feat_b, *filters):
    count = lax.axis_size("arow")
    fits = (
        feat_a.shape == (2, 32, 256)
        and feat_b.shape == (1, 32, 256)
        and count == 16
        and filters[0].shape[0] == 8
    )
    return (fast if fits else general)(feat_a, feat_b, *filters)


def solution(mesh):
    return jax.shard_map(
        on_device,
        mesh=mesh,
        in_specs=(
            P(("groups", "arow"), None, None),
            P(("groups", "arow"), None, None),
            P(),
            P(),
            P(),
            P(),
            P(),
            P(),
        ),
        out_specs=P(("groups", "arow"), None, None),
        check_vma=False,
    )
```

```python
import functools

import jax
import jax.numpy as jnp
from jax import lax
from jax.experimental import pallas as pl
from jax.experimental.pallas import tpu as pltpu
from jax.sharding import PartitionSpec as P

EPSILON = 1e-05
F32 = jnp.float32
BF16 = jnp.bfloat16


def padded(cells, sides, width):
    for axis, dim in sides:
        count = lax.axis_size(axis)
        ends = count - 1
        head = lax.slice_in_dim(cells, 0, width, axis=dim)
        tail = lax.slice_in_dim(cells, cells.shape[dim] - width, cells.shape[dim], axis=dim)
        cells = jnp.concatenate(
            [
                lax.ppermute(tail, axis, [(i, (i + 1) % count) for i in range(ends)]),
                cells,
                lax.ppermute(head, axis, [((i + 1) % count, i) for i in range(ends)]),
            ],
            axis=dim,
        )
    return cells


def shifted_zero(values, along, offset):
    extent = values.shape[along]
    if offset == 0:
        return values
    widths = [(0, 0)] * values.ndim
    if offset > 0:
        widths[along] = (0, offset)
        return lax.slice_in_dim(jnp.pad(values, widths), offset, offset + extent, axis=along)
    widths[along] = (-offset, 0)
    return lax.slice_in_dim(jnp.pad(values, widths), 0, extent, axis=along)


def conv_a(values, kernel):
    out_rows = values.shape[-3] - 2
    result = 0.0
    for row_tap in range(3):
        row_slab = lax.slice_in_dim(
            values, row_tap, row_tap + out_rows, axis=values.ndim - 3
        ).astype(F32)
        for col_tap in range(3):
            result = result + kernel[..., row_tap, col_tap][..., None, None, None] * shifted_zero(
                row_slab, values.ndim - 2, col_tap - 1
            )
    return result


def conv_b(values, kernel, map_width):
    flat_pos = lax.broadcasted_iota(jnp.int32, (values.shape[-1],), 0) % map_width
    result = 0.0
    for row_tap in range(3):
        for col_tap in range(3):
            shifted = shifted_zero(
                values, values.ndim - 1, (row_tap - 1) * map_width + (col_tap - 1)
            )
            inside = ((flat_pos + col_tap - 1 >= 0) & (flat_pos + col_tap - 1 < map_width)).astype(
                F32
            )
            result = result + kernel[..., row_tap, col_tap][..., None, None, None] * (
                shifted * inside
            )
    return result


def first_layer(correlation, kern_a, kern_b, bias_one, map_width):
    spread = conv_a(correlation, kern_a)
    return jax.nn.relu(conv_b(spread, kern_b, map_width) + bias_one[:, None, None, None]).astype(
        BF16
    )


def second_layer(hidden, kern_a, kern_b, bias_two, map_width):
    spread = conv_a(hidden, kern_a)
    summed = jnp.sum(conv_b(spread, kern_b, map_width), axis=0)
    return jax.nn.relu(summed + bias_two[0])


def general(feat_a, feat_b, a_first, b_first, bias_first, a_second, b_second, bias_second):
    map_width = feat_b.shape[1]
    channels = feat_a.shape[2]
    b_cells = feat_b.shape[0] * lax.axis_size("arow") * map_width
    a_rows = feat_a.reshape(-1, channels)
    tile_product = lax.dot_general(
        a_rows,
        lax.all_gather(feat_b, "arow", axis=0, tiled=True).reshape(-1, channels),
        (((1,), (1,)), ((), ())),
        preferred_element_type=F32,
    )
    correlation = (
        (tile_product * channels ** (-0.5))
        .astype(BF16)
        .reshape(feat_a.shape[0], map_width, b_cells)
    )
    correlation = padded(correlation, (("arow", 0),), 1)

    def network(kern_a1, kern_b1, kern_a2, kern_b2):
        hidden = first_layer(correlation, kern_a1, kern_b1, bias_first, map_width)
        hidden = padded(hidden, (("arow", 1),), 1)
        return second_layer(hidden, kern_a2, kern_b2, bias_second, map_width)

    score = network(a_first, b_first, a_second, b_second)
    score = score + network(b_first, a_first, b_second, a_second)
    best_over_a = lax.pmax(jnp.max(score, axis=(0, 1)), "arow")
    best_over_b = jnp.max(score, axis=2)[..., None]
    return score * (score / (best_over_a + EPSILON)) * (score / (best_over_b + EPSILON))


def lane(shape):
    return lax.broadcasted_iota(jnp.int32, shape, 1)


def sublane(shape):
    return lax.broadcasted_iota(jnp.int32, shape, 0)


def two_terms(value):
    high = value.astype(BF16)
    return high, (value - high.astype(F32)).astype(BF16)


def first_weights(taps, at_ref, k, width):
    col = lane((width, 128)) % width
    diag = [sublane((width, 128)) + 1 - col == w for w in range(3)]
    row = lane((1, 128)) // width
    for net in range(2):
        lanes = slice(128 * net, 128 * net + 128)
        for cr in range(6):
            block = jnp.zeros((width, 128), F32)
            for w in range(3):
                per_lane = jnp.zeros((1, 128), F32)
                for u in range(3):
                    if 0 <= cr - u <= 3:
                        per_lane = jnp.where(row == cr - u, taps[net](u, w, k), per_lane)
                block = jnp.where(diag[w], per_lane, block)
            high, low = two_terms(block)
            at_ref[k, cr * width : (cr + 1) * width, lanes] = high
            at_ref[k, (8 + cr) * width : (9 + cr) * width, lanes] = low
        for base in (6, 14):
            at_ref[k, base * width : (base + 2) * width, lanes] = jnp.zeros((2 * width, 128), BF16)


def second_weights(taps, at_ref, k, width, keep):
    col = lane((width, 128)) % width
    diag = [sublane((width, 128)) + 1 - col == w for w in range(3)]
    row = lane((1, 128)) // width
    for net in range(2):
        for hr in range(4):
            block = jnp.zeros((width, 128), F32)
            for w in range(3):
                per_lane = jnp.zeros((1, 128), F32)
                for u in range(3):
                    if 0 <= hr - u <= 1:
                        tap = taps[net](u, w, k)
                        if hr in keep:
                            tap = tap * keep[hr]
                        per_lane = jnp.where(row == 2 * net + hr - u, tap, per_lane)
                block = jnp.where(diag[w], per_lane, block)
            high, low = two_terms(block)
            rows = slice((4 * net + hr) * width, (4 * net + hr + 1) * width)
            at_ref[k, rows, 0:128] = high
            at_ref[k, rows, 128:256] = low


def b_taps(load, weights, emit, width):
    top = sublane((8, 128)) == 0
    bottom = sublane((8, 128)) == 7

    def column(jb):
        even, odd = load(2 * jb), load(2 * jb + 1)
        above = jnp.where(top, 0.0, pltpu.roll(odd, 1, 0))
        below = jnp.where(bottom, 0.0, pltpu.roll(even, 7, 0))
        return above, even, odd, below

    window = [None, column(0), column(1)]
    for jb in range(width):
        sums = []
        for par in range(2):
            total = None
            for t in range(3):
                if window[t] is None:
                    continue
                for s in range(3):
                    term = weights[3 * s + t] * window[t][par + s]
                    total = term if total is None else total + term
            sums.append(total)
        emit(jb, sums[0], sums[1])
        window = [window[1], window[2], column(jb + 2) if jb + 2 < width else None]


def prepare_kernel(width, packed_ref, at1_ref, at2_ref, w1_ref, w2_ref):
    index = lax.axis_index("arow")
    keep = {
        0: (index != 0).astype(F32),
        3: (index != lax.axis_size("arow") - 1).astype(F32),
    }

    def bank(n):
        return lambda u, w, k: packed_ref[3 * n + u, w, k]

    first = (bank(0), bank(1))
    second = (bank(2), bank(3))
    half_lanes = lane((1, 128)) < 64
    for k in range(8):
        first_weights(first, at1_ref, k, width)
        second_weights(second, at2_ref, k, width, keep)
        for tap in range(9):
            at = (tap // 3, tap % 3, k)
            for net in range(2):
                w1_ref[2 * k + net, tap : tap + 1] = jnp.full((1, 128), first[1 - net](*at), F32)
            w2_ref[k, tap : tap + 1] = jnp.where(half_lanes, second[1](*at), second[0](*at))
        for net in range(2):
            w1_ref[2 * k + net, 9:10] = jnp.full((1, 128), packed_ref[12, 0, k], F32)


def pack(bias, *banks):
    packed = jnp.pad(bias.reshape(1, 1, 8), ((12, 0), (0, 2), (0, 0)))
    for n, f in enumerate(banks):
        packed += jnp.pad(f.transpose(1, 2, 0), ((3 * n, 10 - 3 * n), (0, 0), (0, 0)))
    return packed


def prepare(packed, width):
    vmem = pl.BlockSpec(memory_space=pltpu.VMEM)
    return pl.pallas_call(
        functools.partial(prepare_kernel, width),
        out_shape=(
            jax.ShapeDtypeStruct((8, 512, 256), BF16),
            jax.ShapeDtypeStruct((8, 256, 256), BF16),
            jax.ShapeDtypeStruct((16, 16, 128), F32),
            jax.ShapeDtypeStruct((8, 16, 128), F32),
        ),
        in_specs=[pl.BlockSpec(memory_space=pltpu.SMEM)],
        out_specs=(vmem,) * 4,
        compiler_params=pltpu.CompilerParams(vmem_limit_bytes=16 << 20),
        cost_estimate=pl.CostEstimate(
            flops=4_000_000, bytes_accessed=3_500_000, transcendentals=0
        ),
    )(packed)


def consensus_kernel(
    offsets,
    width,
    bias2_ref,
    at1_ref,
    at2_ref,
    w1_ref,
    w2_ref,
    own_ref,
    mate_ref,
    outer_ref,
    score_ref,
    part_ref,
    best_ref,
    fa_ref,
    vf_ref,
    vp_ref,
    s_ref,
    h_ref,
    t_ref,
    acc_ref,
    nat_ref,
):
    half = len(offsets)
    channels = own_ref.shape[2]
    index = lax.axis_index("arow")
    parity = index % 2
    inside = jnp.logical_and(index != 0, index != lax.axis_size("arow") - 1)

    fa_ref[2:4] = own_ref[half : half + 2]
    fa_ref[pl.ds(4 - 4 * parity, 2)] = mate_ref[half : half + 2]
    fa_ref[pl.ds(4 * parity, 2)] = outer_ref[...] * inside.astype(BF16)
    fa_ref[6:8] = jnp.zeros((2, width, channels), BF16)
    rows = fa_ref[...].reshape(8 * width, channels)

    for side, ref in enumerate((own_ref, mate_ref)):
        product = lax.dot_general(
            ref[0:half].reshape(half * width, channels),
            rows,
            (((1,), (1,)), ((), ())),
            preferred_element_type=F32,
        )
        for g in range(half):
            ib = index ^ (offsets[g] ^ side)
            start = (ib % 2) * 8 + ib // 2
            block = product[g * width : (g + 1) * width] * channels ** (-0.5)
            for c in range(2):
                vf_ref[c, pl.ds(start, width, stride=16), :] = block[
                    :, 128 * c : 128 * c + 128
                ]
    for c in range(4):
        vp_ref[:, 128 * c : 128 * c + 128] = vf_ref[c % 2].astype(BF16)

    for k in range(8):
        s_ref[k % 2] = jnp.dot(vp_ref[...], at1_ref[k], preferred_element_type=F32)
        for net in range(2):
            weights = [w1_ref[2 * k + net, tap : tap + 1] for tap in range(9)]
            bias = w1_ref[2 * k + net, 9:10]

            def load(r, net=net, k=k):
                return s_ref[k % 2, 8 * r : 8 * r + 8, 128 * net : 128 * net + 128]

            def emit(jb, even, odd, net=net, k=k, bias=bias):
                pair = jnp.concatenate([even, odd], axis=0)
                h_ref[k % 2, 16 * jb : 16 * jb + 16, 128 * net : 128 * net + 128] = jnp.maximum(
                    pair + bias, 0.0
                ).astype(BF16)

            b_taps(load, weights, emit, width)
        both = jnp.dot(h_ref[k % 2], at2_ref[k], preferred_element_type=F32)
        t_ref[k % 2] = both[:, 0:128] + both[:, 128:256]
        weights = [w2_ref[k, tap : tap + 1] for tap in range(9)]

        def load(r, k=k):
            return t_ref[k % 2, 8 * r : 8 * r + 8, :]

        def emit(jb, even, odd, k=k):
            pair = jnp.concatenate([even, odd], axis=0)
            if k == 0:
                acc_ref[16 * jb : 16 * jb + 16, :] = pair
            elif k < 7:
                acc_ref[16 * jb : 16 * jb + 16, :] += pair
            else:
                total = jnp.maximum(
                    acc_ref[16 * jb : 16 * jb + 16, :] + pair + bias2_ref[0], 0.0
                )
                nat_ref[pl.ds(jb, 8, stride=2 * width), :] = total[0:8]
                nat_ref[pl.ds(width + jb, 8, stride=2 * width), :] = total[8:16]

        b_taps(load, weights, emit, width)

    turned = jnp.transpose(nat_ref[...], (1, 0))
    score = turned[0:64] + turned[64:128]
    best_ref[...] = jnp.max(score, axis=0, keepdims=True)
    best_b = jnp.max(score, axis=1, keepdims=True)
    score_ref[...] = score
    part_ref[...] = score * (score / (best_b + EPSILON))


def consensus(bias_second, weights, own, mate, outer, offsets, width):
    half = len(offsets)
    cells = 2 * half * width
    channels = own.shape[2]
    vmem = pl.BlockSpec(memory_space=pltpu.VMEM)
    return pl.pallas_call(
        functools.partial(consensus_kernel, offsets, width),
        out_shape=(
            jax.ShapeDtypeStruct((2 * width, cells), F32),
            jax.ShapeDtypeStruct((2 * width, cells), F32),
            jax.ShapeDtypeStruct((1, cells), F32),
        ),
        in_specs=[pl.BlockSpec(memory_space=pltpu.SMEM)] + [vmem] * 7,
        out_specs=(vmem, vmem, vmem),
        scratch_shapes=[
            pltpu.VMEM((8, width, channels), BF16),
            pltpu.VMEM((2, cells, 128), F32),
            pltpu.VMEM((cells, 512), BF16),
            pltpu.VMEM((2, cells, 256), F32),
            pltpu.VMEM((2, cells, 256), BF16),
            pltpu.VMEM((2, cells, 128), F32),
            pltpu.VMEM((cells, 128), F32),
            pltpu.VMEM((cells, 128), F32),
        ],
        compiler_params=pltpu.CompilerParams(vmem_limit_bytes=32 << 20),
        cost_estimate=pl.CostEstimate(
            flops=2_000_000_000, bytes_accessed=4_500_000, transcendentals=0
        ),
    )(bias_second, *weights, own, mate, outer)


def exchange(value, mask, count):
    return lax.ppermute(value, "arow", [(i, i ^ mask) for i in range(count)])


def outer_pairs(groups, count):
    pairs = []
    for g in range(groups):
        for i in range(count):
            j = i + 1 if i % 2 else i - 1
            if 0 <= j < count:
                pairs.append((g * count + i, g * count + j))
            else:
                other = g ^ 1 if (g ^ 1) < groups else g
                pairs.append((g * count + i, other * count + i))
    return pairs


def fast(feat_a, feat_b, a_first, b_first, bias_first, a_second, b_second, bias_second):
    count = lax.axis_size("arow")
    groups = lax.axis_size("groups")
    width = feat_b.shape[1]
    masks = [(1 << b) | 1 for b in reversed(range(1, count.bit_length() - 1))]

    rows = feat_a.shape[0]
    near = lax.optimization_barrier(jnp.concatenate([feat_a, feat_b], axis=0))
    near_a, near_b = near[:rows], near[rows:]
    packed = pack(bias_first, a_first, b_first, a_second, b_second)
    held, offsets = feat_b, [0]
    for n, mask in enumerate(masks):
        if n == 1:
            held, packed = lax.optimization_barrier((held, packed))
            weights = prepare(packed, width)
        if n == 2:
            feat_a, held, weights = lax.optimization_barrier((feat_a, held, weights))
            outer = lax.ppermute(feat_a, ("groups", "arow"), outer_pairs(groups, count))
        received = exchange(held, mask, count)
        held = jnp.concatenate([near_b if n == 0 else held, received], axis=0)
        offsets = offsets + [o ^ mask for o in offsets]
    held, outer, bias_second = lax.optimization_barrier((held, outer, bias_second))
    own = jnp.concatenate([held, near_a], axis=0)
    mate = exchange(own, 1, count)

    score, part, best = consensus(bias_second, weights, own, mate, outer, offsets, width)
    for mask in masks + [1]:
        best = jnp.maximum(best, exchange(best, mask, count))
    out = part * (score / (best + EPSILON))
    return out.reshape(feat_a.shape[0], width, -1)


def on_device(feat_a, feat_b, *filters):
    count = lax.axis_size("arow")
    fits = (
        feat_a.shape == (2, 32, 256)
        and feat_b.shape == (1, 32, 256)
        and count == 16
        and filters[0].shape[0] == 8
    )
    return (fast if fits else general)(feat_a, feat_b, *filters)


def solution(mesh):
    return jax.shard_map(
        on_device,
        mesh=mesh,
        in_specs=(
            P(("groups", "arow"), None, None),
            P(("groups", "arow"), None, None),
            P(),
            P(),
            P(),
            P(),
            P(),
            P(),
        ),
        out_specs=P(("groups", "arow"), None, None),
        check_vma=False,
    )
```

```python
import functools

import jax
import jax.numpy as jnp
from jax import lax
from jax.experimental import pallas as pl
from jax.experimental.pallas import tpu as pltpu
from jax.sharding import PartitionSpec as P

EPSILON = 1e-05
F32 = jnp.float32
BF16 = jnp.bfloat16


def padded(cells, sides, width):
    for axis, dim in sides:
        count = lax.axis_size(axis)
        ends = count - 1
        head = lax.slice_in_dim(cells, 0, width, axis=dim)
        tail = lax.slice_in_dim(cells, cells.shape[dim] - width, cells.shape[dim], axis=dim)
        cells = jnp.concatenate(
            [
                lax.ppermute(tail, axis, [(i, (i + 1) % count) for i in range(ends)]),
                cells,
                lax.ppermute(head, axis, [((i + 1) % count, i) for i in range(ends)]),
            ],
            axis=dim,
        )
    return cells


def shifted_zero(values, along, offset):
    extent = values.shape[along]
    if offset == 0:
        return values
    widths = [(0, 0)] * values.ndim
    if offset > 0:
        widths[along] = (0, offset)
        return lax.slice_in_dim(jnp.pad(values, widths), offset, offset + extent, axis=along)
    widths[along] = (-offset, 0)
    return lax.slice_in_dim(jnp.pad(values, widths), 0, extent, axis=along)


def conv_a(values, kernel):
    out_rows = values.shape[-3] - 2
    result = 0.0
    for row_tap in range(3):
        row_slab = lax.slice_in_dim(
            values, row_tap, row_tap + out_rows, axis=values.ndim - 3
        ).astype(F32)
        for col_tap in range(3):
            result = result + kernel[..., row_tap, col_tap][..., None, None, None] * shifted_zero(
                row_slab, values.ndim - 2, col_tap - 1
            )
    return result


def conv_b(values, kernel, map_width):
    flat_pos = lax.broadcasted_iota(jnp.int32, (values.shape[-1],), 0) % map_width
    result = 0.0
    for row_tap in range(3):
        for col_tap in range(3):
            shifted = shifted_zero(
                values, values.ndim - 1, (row_tap - 1) * map_width + (col_tap - 1)
            )
            inside = ((flat_pos + col_tap - 1 >= 0) & (flat_pos + col_tap - 1 < map_width)).astype(
                F32
            )
            result = result + kernel[..., row_tap, col_tap][..., None, None, None] * (
                shifted * inside
            )
    return result


def first_layer(correlation, kern_a, kern_b, bias_one, map_width):
    spread = conv_a(correlation, kern_a)
    return jax.nn.relu(conv_b(spread, kern_b, map_width) + bias_one[:, None, None, None]).astype(
        BF16
    )


def second_layer(hidden, kern_a, kern_b, bias_two, map_width):
    spread = conv_a(hidden, kern_a)
    summed = jnp.sum(conv_b(spread, kern_b, map_width), axis=0)
    return jax.nn.relu(summed + bias_two[0])


def general(feat_a, feat_b, a_first, b_first, bias_first, a_second, b_second, bias_second):
    map_width = feat_b.shape[1]
    channels = feat_a.shape[2]
    b_cells = feat_b.shape[0] * lax.axis_size("arow") * map_width
    a_rows = feat_a.reshape(-1, channels)
    tile_product = lax.dot_general(
        a_rows,
        lax.all_gather(feat_b, "arow", axis=0, tiled=True).reshape(-1, channels),
        (((1,), (1,)), ((), ())),
        preferred_element_type=F32,
    )
    correlation = (
        (tile_product * channels ** (-0.5))
        .astype(BF16)
        .reshape(feat_a.shape[0], map_width, b_cells)
    )
    correlation = padded(correlation, (("arow", 0),), 1)

    def network(kern_a1, kern_b1, kern_a2, kern_b2):
        hidden = first_layer(correlation, kern_a1, kern_b1, bias_first, map_width)
        hidden = padded(hidden, (("arow", 1),), 1)
        return second_layer(hidden, kern_a2, kern_b2, bias_second, map_width)

    score = network(a_first, b_first, a_second, b_second)
    score = score + network(b_first, a_first, b_second, a_second)
    best_over_a = lax.pmax(jnp.max(score, axis=(0, 1)), "arow")
    best_over_b = jnp.max(score, axis=2)[..., None]
    return score * (score / (best_over_a + EPSILON)) * (score / (best_over_b + EPSILON))


def lane(shape):
    return lax.broadcasted_iota(jnp.int32, shape, 1)


def sublane(shape):
    return lax.broadcasted_iota(jnp.int32, shape, 0)


def two_terms(value):
    high = value.astype(BF16)
    return high, (value - high.astype(F32)).astype(BF16)


def first_weights(taps, at_ref, k, width):
    col = lane((width, 128)) % width
    diag = [sublane((width, 128)) + 1 - col == w for w in range(3)]
    row = lane((1, 128)) // width
    for net in range(2):
        lanes = slice(128 * net, 128 * net + 128)
        for cr in range(6):
            block = jnp.zeros((width, 128), F32)
            for w in range(3):
                per_lane = jnp.zeros((1, 128), F32)
                for u in range(3):
                    if 0 <= cr - u <= 3:
                        per_lane = jnp.where(row == cr - u, taps[net](u, w, k), per_lane)
                block = jnp.where(diag[w], per_lane, block)
            high, low = two_terms(block)
            at_ref[k, cr * width : (cr + 1) * width, lanes] = high
            at_ref[k, (8 + cr) * width : (9 + cr) * width, lanes] = low
        for base in (6, 14):
            at_ref[k, base * width : (base + 2) * width, lanes] = jnp.zeros((2 * width, 128), BF16)


def second_weights(taps, at_ref, k, width, keep):
    col = lane((width, 128)) % width
    diag = [sublane((width, 128)) + 1 - col == w for w in range(3)]
    row = lane((1, 128)) // width
    for net in range(2):
        for hr in range(4):
            block = jnp.zeros((width, 128), F32)
            for w in range(3):
                per_lane = jnp.zeros((1, 128), F32)
                for u in range(3):
                    if 0 <= hr - u <= 1:
                        tap = taps[net](u, w, k)
                        if hr in keep:
                            tap = tap * keep[hr]
                        per_lane = jnp.where(row == 2 * net + hr - u, tap, per_lane)
                block = jnp.where(diag[w], per_lane, block)
            high, low = two_terms(block)
            rows = slice((4 * net + hr) * width, (4 * net + hr + 1) * width)
            at_ref[k, rows, 0:128] = high
            at_ref[k, rows, 128:256] = low


def b_taps(load, weights, emit, width):
    top = sublane((8, 128)) == 0
    bottom = sublane((8, 128)) == 7

    def column(jb):
        even, odd = load(2 * jb), load(2 * jb + 1)
        above = jnp.where(top, 0.0, pltpu.roll(odd, 1, 0))
        below = jnp.where(bottom, 0.0, pltpu.roll(even, 7, 0))
        return above, even, odd, below

    window = [None, column(0), column(1)]
    for jb in range(width):
        sums = []
        for par in range(2):
            total = None
            for t in range(3):
                if window[t] is None:
                    continue
                for s in range(3):
                    term = weights[3 * s + t] * window[t][par + s]
                    total = term if total is None else total + term
            sums.append(total)
        emit(jb, sums[0], sums[1])
        yield
        window = [window[1], window[2], column(jb + 2) if jb + 2 < width else None]


def prepare_kernel(width, packed_ref, at1_ref, at2_ref, w1_ref, w2_ref):
    index = lax.axis_index("arow")
    keep = {
        0: (index != 0).astype(F32),
        3: (index != lax.axis_size("arow") - 1).astype(F32),
    }

    def bank(n):
        return lambda u, w, k: packed_ref[3 * n + u, w, k]

    first = (bank(0), bank(1))
    second = (bank(2), bank(3))
    half_lanes = lane((1, 128)) < 64
    for k in range(8):
        first_weights(first, at1_ref, k, width)
        second_weights(second, at2_ref, k, width, keep)
        for tap in range(9):
            at = (tap // 3, tap % 3, k)
            for net in range(2):
                w1_ref[2 * k + net, tap : tap + 1] = jnp.full((1, 128), first[1 - net](*at), F32)
            w2_ref[k, tap : tap + 1] = jnp.where(half_lanes, second[1](*at), second[0](*at))
        for net in range(2):
            w1_ref[2 * k + net, 9:10] = jnp.full((1, 128), packed_ref[12, 0, k], F32)


def pack(bias, *banks):
    packed = jnp.pad(bias.reshape(1, 1, 8), ((12, 0), (0, 2), (0, 0)))
    for n, f in enumerate(banks):
        packed += jnp.pad(f.transpose(1, 2, 0), ((3 * n, 10 - 3 * n), (0, 0), (0, 0)))
    return packed


def prepare(packed, width):
    vmem = pl.BlockSpec(memory_space=pltpu.VMEM)
    return pl.pallas_call(
        functools.partial(prepare_kernel, width),
        out_shape=(
            jax.ShapeDtypeStruct((8, 512, 256), BF16),
            jax.ShapeDtypeStruct((8, 256, 256), BF16),
            jax.ShapeDtypeStruct((16, 16, 128), F32),
            jax.ShapeDtypeStruct((8, 16, 128), F32),
        ),
        in_specs=[pl.BlockSpec(memory_space=pltpu.SMEM)],
        out_specs=(vmem,) * 4,
        compiler_params=pltpu.CompilerParams(vmem_limit_bytes=16 << 20),
        cost_estimate=pl.CostEstimate(
            flops=500_000_000, bytes_accessed=3_500_000, transcendentals=0
        ),
    )(packed)


def consensus_kernel(
    offsets,
    width,
    bias2_ref,
    at1_ref,
    at2_ref,
    w1_ref,
    w2_ref,
    own_ref,
    mate_ref,
    outer_ref,
    score_ref,
    part_ref,
    best_ref,
    fa_ref,
    vf_ref,
    vp_ref,
    s_ref,
    h_ref,
    t_ref,
    acc_ref,
    nat_ref,
):
    half = len(offsets)
    channels = own_ref.shape[2]
    index = lax.axis_index("arow")
    parity = index % 2
    inside = jnp.logical_and(index != 0, index != lax.axis_size("arow") - 1)

    fa_ref[2:4] = own_ref[half : half + 2]
    fa_ref[pl.ds(4 - 4 * parity, 2)] = mate_ref[half : half + 2]
    fa_ref[pl.ds(4 * parity, 2)] = outer_ref[...] * inside.astype(BF16)
    fa_ref[6:8] = jnp.zeros((2, width, channels), BF16)
    rows = fa_ref[...].reshape(8 * width, channels)

    for side, ref in enumerate((own_ref, mate_ref)):
        product = lax.dot_general(
            ref[0:half].reshape(half * width, channels),
            rows,
            (((1,), (1,)), ((), ())),
            preferred_element_type=F32,
        )
        for g in range(half):
            ib = index ^ (offsets[g] ^ side)
            start = (ib % 2) * 8 + ib // 2
            block = product[g * width : (g + 1) * width] * channels ** (-0.5)
            for c in range(2):
                vf_ref[c, pl.ds(start, width, stride=16), :] = block[
                    :, 128 * c : 128 * c + 128
                ]
    for c in range(4):
        vp_ref[:, 128 * c : 128 * c + 128] = vf_ref[c % 2].astype(BF16)

    def spread(k):
        s_ref[k % 2] = jnp.dot(vp_ref[...], at1_ref[k], preferred_element_type=F32)

    def hide(k):
        for net in range(2):
            weights = [w1_ref[2 * k + net, tap : tap + 1] for tap in range(9)]
            bias = w1_ref[2 * k + net, 9:10]

            def load(r):
                return s_ref[k % 2, 8 * r : 8 * r + 8, 128 * net : 128 * net + 128]

            def emit(jb, even, odd):
                pair = jnp.concatenate([even, odd], axis=0)
                h_ref[k % 2, 16 * jb : 16 * jb + 16, 128 * net : 128 * net + 128] = jnp.maximum(
                    pair + bias, 0.0
                ).astype(BF16)

            yield from b_taps(load, weights, emit, width)

    def gather_rows(k):
        both = jnp.dot(h_ref[k % 2], at2_ref[k], preferred_element_type=F32)
        t_ref[k % 2] = both[:, 0:128] + both[:, 128:256]

    def gather_taps(k):
        weights = [w2_ref[k, tap : tap + 1] for tap in range(9)]

        def load(r):
            return t_ref[k % 2, 8 * r : 8 * r + 8, :]

        def emit(jb, even, odd):
            pair = jnp.concatenate([even, odd], axis=0)
            if k == 0:
                acc_ref[16 * jb : 16 * jb + 16, :] = pair
            elif k < 7:
                acc_ref[16 * jb : 16 * jb + 16, :] += pair
            else:
                total = jnp.maximum(
                    acc_ref[16 * jb : 16 * jb + 16, :] + pair + bias2_ref[0], 0.0
                )
                nat_ref[pl.ds(jb, 8, stride=2 * width), :] = total[0:8]
                nat_ref[pl.ds(width + jb, 8, stride=2 * width), :] = total[8:16]

        yield from b_taps(load, weights, emit, width)

    for step in range(11):
        if step < 8:
            spread(step)
        if 2 <= step < 10:
            gather_rows(step - 2)
        ones = hide(step - 1) if 1 <= step < 9 else iter(())
        twos = gather_taps(step - 3) if step >= 3 else iter(())
        for _ in range(width):
            next(ones, None)
            next(twos, None)
            next(ones, None)

    turned = jnp.transpose(nat_ref[...], (1, 0))
    score = turned[0:64] + turned[64:128]
    best_ref[...] = jnp.max(score, axis=0, keepdims=True)
    best_b = jnp.max(score, axis=1, keepdims=True)
    score_ref[...] = score
    part_ref[...] = score * (score / (best_b + EPSILON))


def consensus(bias_second, weights, own, mate, outer, offsets, width):
    half = len(offsets)
    cells = 2 * half * width
    channels = own.shape[2]
    vmem = pl.BlockSpec(memory_space=pltpu.VMEM)
    return pl.pallas_call(
        functools.partial(consensus_kernel, offsets, width),
        out_shape=(
            jax.ShapeDtypeStruct((2 * width, cells), F32),
            jax.ShapeDtypeStruct((2 * width, cells), F32),
            jax.ShapeDtypeStruct((1, cells), F32),
        ),
        in_specs=[pl.BlockSpec(memory_space=pltpu.SMEM)] + [vmem] * 7,
        out_specs=(vmem, vmem, vmem),
        scratch_shapes=[
            pltpu.VMEM((8, width, channels), BF16),
            pltpu.VMEM((2, cells, 128), F32),
            pltpu.VMEM((cells, 512), BF16),
            pltpu.VMEM((2, cells, 256), F32),
            pltpu.VMEM((2, cells, 256), BF16),
            pltpu.VMEM((2, cells, 128), F32),
            pltpu.VMEM((cells, 128), F32),
            pltpu.VMEM((cells, 128), F32),
        ],
        compiler_params=pltpu.CompilerParams(vmem_limit_bytes=32 << 20),
        cost_estimate=pl.CostEstimate(
            flops=2_000_000_000, bytes_accessed=4_500_000, transcendentals=0
        ),
    )(bias_second, *weights, own, mate, outer)


def exchange(value, mask, count):
    return lax.ppermute(value, "arow", [(i, i ^ mask) for i in range(count)])


def outer_pairs(groups, count):
    pairs = []
    for g in range(groups):
        for i in range(count):
            j = i + 1 if i % 2 else i - 1
            if 0 <= j < count:
                pairs.append((g * count + i, g * count + j))
            else:
                other = g ^ 1 if (g ^ 1) < groups else g
                pairs.append((g * count + i, other * count + i))
    return pairs


def fast(feat_a, feat_b, a_first, b_first, bias_first, a_second, b_second, bias_second):
    count = lax.axis_size("arow")
    groups = lax.axis_size("groups")
    width = feat_b.shape[1]
    masks = [(1 << b) | 1 for b in reversed(range(1, count.bit_length() - 1))]

    rows = feat_a.shape[0]
    near = lax.optimization_barrier(jnp.concatenate([feat_a, feat_b], axis=0))
    near_a, near_b = near[:rows], near[rows:]
    packed = pack(bias_first, a_first, b_first, a_second, b_second)
    held, offsets = feat_b, [0]
    for n, mask in enumerate(masks):
        if n == 1:
            feat_a, held, packed = lax.optimization_barrier((feat_a, held, packed))
            outer = lax.ppermute(feat_a, ("groups", "arow"), outer_pairs(groups, count))
        if n == 2:
            packed, outer = lax.optimization_barrier((packed, outer))
            weights = prepare(packed, width)
        received = exchange(held, mask, count)
        held = jnp.concatenate([near_b if n == 0 else held, received], axis=0)
        offsets = offsets + [o ^ mask for o in offsets]
    held, outer, weights, bias_second = lax.optimization_barrier(
        (held, outer, weights, bias_second)
    )
    own = jnp.concatenate([held, near_a], axis=0)
    mate = exchange(own, 1, count)

    score, part, best = consensus(bias_second, weights, own, mate, outer, offsets, width)
    for mask in masks + [1]:
        best = jnp.maximum(best, exchange(best, mask, count))
    out = part * (score / (best + EPSILON))
    return out.reshape(feat_a.shape[0], width, -1)


def on_device(feat_a, feat_b, *filters):
    count = lax.axis_size("arow")
    fits = (
        feat_a.shape == (2, 32, 256)
        and feat_b.shape == (1, 32, 256)
        and count == 16
        and filters[0].shape[0] == 8
    )
    return (fast if fits else general)(feat_a, feat_b, *filters)


def solution(mesh):
    return jax.shard_map(
        on_device,
        mesh=mesh,
        in_specs=(
            P(("groups", "arow"), None, None),
            P(("groups", "arow"), None, None),
            P(),
            P(),
            P(),
            P(),
            P(),
            P(),
        ),
        out_specs=P(("groups", "arow"), None, None),
        check_vma=False,
    )
```

```python
import functools

import jax
import jax.numpy as jnp
from jax import lax
from jax.experimental import pallas as pl
from jax.experimental.pallas import tpu as pltpu
from jax.sharding import PartitionSpec as P

EPSILON = 1e-05
F32 = jnp.float32
BF16 = jnp.bfloat16


def padded(cells, sides, width):
    for axis, dim in sides:
        count = lax.axis_size(axis)
        ends = count - 1
        head = lax.slice_in_dim(cells, 0, width, axis=dim)
        tail = lax.slice_in_dim(cells, cells.shape[dim] - width, cells.shape[dim], axis=dim)
        cells = jnp.concatenate(
            [
                lax.ppermute(tail, axis, [(i, (i + 1) % count) for i in range(ends)]),
                cells,
                lax.ppermute(head, axis, [((i + 1) % count, i) for i in range(ends)]),
            ],
            axis=dim,
        )
    return cells


def shifted_zero(values, along, offset):
    extent = values.shape[along]
    if offset == 0:
        return values
    widths = [(0, 0)] * values.ndim
    if offset > 0:
        widths[along] = (0, offset)
        return lax.slice_in_dim(jnp.pad(values, widths), offset, offset + extent, axis=along)
    widths[along] = (-offset, 0)
    return lax.slice_in_dim(jnp.pad(values, widths), 0, extent, axis=along)


def conv_a(values, kernel):
    out_rows = values.shape[-3] - 2
    result = 0.0
    for row_tap in range(3):
        row_slab = lax.slice_in_dim(
            values, row_tap, row_tap + out_rows, axis=values.ndim - 3
        ).astype(F32)
        for col_tap in range(3):
            result = result + kernel[..., row_tap, col_tap][..., None, None, None] * shifted_zero(
                row_slab, values.ndim - 2, col_tap - 1
            )
    return result


def conv_b(values, kernel, map_width):
    flat_pos = lax.broadcasted_iota(jnp.int32, (values.shape[-1],), 0) % map_width
    result = 0.0
    for row_tap in range(3):
        for col_tap in range(3):
            shifted = shifted_zero(
                values, values.ndim - 1, (row_tap - 1) * map_width + (col_tap - 1)
            )
            inside = ((flat_pos + col_tap - 1 >= 0) & (flat_pos + col_tap - 1 < map_width)).astype(
                F32
            )
            result = result + kernel[..., row_tap, col_tap][..., None, None, None] * (
                shifted * inside
            )
    return result


def first_layer(correlation, kern_a, kern_b, bias_one, map_width):
    spread = conv_a(correlation, kern_a)
    return jax.nn.relu(conv_b(spread, kern_b, map_width) + bias_one[:, None, None, None]).astype(
        BF16
    )


def second_layer(hidden, kern_a, kern_b, bias_two, map_width):
    spread = conv_a(hidden, kern_a)
    summed = jnp.sum(conv_b(spread, kern_b, map_width), axis=0)
    return jax.nn.relu(summed + bias_two[0])


def general(feat_a, feat_b, a_first, b_first, bias_first, a_second, b_second, bias_second):
    map_width = feat_b.shape[1]
    channels = feat_a.shape[2]
    b_cells = feat_b.shape[0] * lax.axis_size("arow") * map_width
    a_rows = feat_a.reshape(-1, channels)
    tile_product = lax.dot_general(
        a_rows,
        lax.all_gather(feat_b, "arow", axis=0, tiled=True).reshape(-1, channels),
        (((1,), (1,)), ((), ())),
        preferred_element_type=F32,
    )
    correlation = (
        (tile_product * channels ** (-0.5))
        .astype(BF16)
        .reshape(feat_a.shape[0], map_width, b_cells)
    )
    correlation = padded(correlation, (("arow", 0),), 1)

    def network(kern_a1, kern_b1, kern_a2, kern_b2):
        hidden = first_layer(correlation, kern_a1, kern_b1, bias_first, map_width)
        hidden = padded(hidden, (("arow", 1),), 1)
        return second_layer(hidden, kern_a2, kern_b2, bias_second, map_width)

    score = network(a_first, b_first, a_second, b_second)
    score = score + network(b_first, a_first, b_second, a_second)
    best_over_a = lax.pmax(jnp.max(score, axis=(0, 1)), "arow")
    best_over_b = jnp.max(score, axis=2)[..., None]
    return score * (score / (best_over_a + EPSILON)) * (score / (best_over_b + EPSILON))


def lane(shape):
    return lax.broadcasted_iota(jnp.int32, shape, 1)


def sublane(shape):
    return lax.broadcasted_iota(jnp.int32, shape, 0)


def two_terms(value):
    high = value.astype(BF16)
    return high, (value - high.astype(F32)).astype(BF16)


def first_weights(taps, at_ref, k, width):
    col = lane((width, 128)) % width
    diag = [sublane((width, 128)) + 1 - col == w for w in range(3)]
    row = lane((1, 128)) // width
    for net in range(2):
        lanes = slice(128 * net, 128 * net + 128)
        for cr in range(6):
            block = jnp.zeros((width, 128), F32)
            for w in range(3):
                per_lane = jnp.zeros((1, 128), F32)
                for u in range(3):
                    if 0 <= cr - u <= 3:
                        per_lane = jnp.where(row == cr - u, taps[net](u, w, k), per_lane)
                block = jnp.where(diag[w], per_lane, block)
            high, low = two_terms(block)
            at_ref[k, cr * width : (cr + 1) * width, lanes] = high
            at_ref[k, (8 + cr) * width : (9 + cr) * width, lanes] = low
        for base in (6, 14):
            at_ref[k, base * width : (base + 2) * width, lanes] = jnp.zeros((2 * width, 128), BF16)


def second_weights(taps, at_ref, k, width, keep):
    col = lane((width, 128)) % width
    diag = [sublane((width, 128)) + 1 - col == w for w in range(3)]
    row = lane((1, 128)) // width
    for net in range(2):
        for hr in range(4):
            block = jnp.zeros((width, 128), F32)
            for w in range(3):
                per_lane = jnp.zeros((1, 128), F32)
                for u in range(3):
                    if 0 <= hr - u <= 1:
                        tap = taps[net](u, w, k)
                        if hr in keep:
                            tap = tap * keep[hr]
                        per_lane = jnp.where(row == 2 * net + hr - u, tap, per_lane)
                block = jnp.where(diag[w], per_lane, block)
            high, low = two_terms(block)
            rows = slice((4 * net + hr) * width, (4 * net + hr + 1) * width)
            at_ref[k, rows, 0:128] = high
            at_ref[k, rows, 128:256] = low


def minimal_filter(taps):
    parts = [[], [], [], []]
    for t in range(3):
        ends = 0.5 * (taps[t] + taps[6 + t])
        middle = 0.5 * taps[3 + t]
        for part, row in zip(parts, (taps[t], ends + middle, ends - middle, taps[6 + t])):
            part.append(row)
    return sum(parts, [])


def b_taps(load, weights, emit, width):
    top = sublane((8, 128)) == 0
    bottom = sublane((8, 128)) == 7

    def column(jb):
        even, odd = load(2 * jb), load(2 * jb + 1)
        above = jnp.where(top, 0.0, pltpu.roll(odd, 1, 0))
        below = jnp.where(bottom, 0.0, pltpu.roll(even, 7, 0))
        return above - odd, even + odd, odd - even, even - below

    window = [None, column(0), column(1)]
    for jb in range(width):
        sums = []
        for part in range(4):
            total = None
            for t in range(3):
                if window[t] is None:
                    continue
                term = weights[3 * part + t] * window[t][part]
                total = term if total is None else total + term
            sums.append(total)
        emit(jb, sums)
        yield
        window = [window[1], window[2], column(jb + 2) if jb + 2 < width else None]


def pair_of(sums):
    first, second, third, fourth = sums
    return jnp.concatenate([first + second + third, second - third - fourth], axis=0)


def prepare_kernel(width, packed_ref, at1_ref, at2_ref, w1_ref, w2_ref):
    index = lax.axis_index("arow")
    keep = {
        0: (index != 0).astype(F32),
        3: (index != lax.axis_size("arow") - 1).astype(F32),
    }

    def bank(n):
        return lambda u, w, k: packed_ref[3 * n + u, w, k]

    first = (bank(0), bank(1))
    second = (bank(2), bank(3))
    half_lanes = lane((1, 128)) < 64
    for k in range(8):
        first_weights(first, at1_ref, k, width)
        second_weights(second, at2_ref, k, width, keep)
        places = [(tap // 3, tap % 3, k) for tap in range(9)]
        for net in range(2):
            rows = minimal_filter([jnp.full((1, 128), first[1 - net](*at), F32) for at in places])
            for n, row in enumerate(rows):
                w1_ref[2 * k + net, n : n + 1] = row
            w1_ref[2 * k + net, 12:13] = jnp.full((1, 128), packed_ref[12, 0, k], F32)
        rows = minimal_filter(
            [jnp.where(half_lanes, second[1](*at), second[0](*at)) for at in places]
        )
        for n, row in enumerate(rows):
            w2_ref[k, n : n + 1] = row


def pack(bias, *banks):
    packed = jnp.pad(bias.reshape(1, 1, 8), ((12, 0), (0, 2), (0, 0)))
    for n, f in enumerate(banks):
        packed += jnp.pad(f.transpose(1, 2, 0), ((3 * n, 10 - 3 * n), (0, 0), (0, 0)))
    return packed


def prepare(packed, width):
    vmem = pl.BlockSpec(memory_space=pltpu.VMEM)
    return pl.pallas_call(
        functools.partial(prepare_kernel, width),
        out_shape=(
            jax.ShapeDtypeStruct((8, 512, 256), BF16),
            jax.ShapeDtypeStruct((8, 256, 256), BF16),
            jax.ShapeDtypeStruct((16, 16, 128), F32),
            jax.ShapeDtypeStruct((8, 16, 128), F32),
        ),
        in_specs=[pl.BlockSpec(memory_space=pltpu.SMEM)],
        out_specs=(vmem,) * 4,
        compiler_params=pltpu.CompilerParams(vmem_limit_bytes=16 << 20),
        cost_estimate=pl.CostEstimate(
            flops=500_000_000, bytes_accessed=3_500_000, transcendentals=0
        ),
    )(packed)


def consensus_kernel(
    offsets,
    width,
    bias2_ref,
    at1_ref,
    at2_ref,
    w1_ref,
    w2_ref,
    own_ref,
    mate_ref,
    outer_ref,
    score_ref,
    part_ref,
    best_ref,
    fa_ref,
    vf_ref,
    vp_ref,
    s_ref,
    h_ref,
    t_ref,
    acc_ref,
    nat_ref,
):
    half = len(offsets)
    channels = own_ref.shape[2]
    index = lax.axis_index("arow")
    parity = index % 2
    inside = jnp.logical_and(index != 0, index != lax.axis_size("arow") - 1)

    fa_ref[2:4] = own_ref[half : half + 2]
    fa_ref[pl.ds(4 - 4 * parity, 2)] = mate_ref[half : half + 2]
    fa_ref[pl.ds(4 * parity, 2)] = outer_ref[...] * inside.astype(BF16)
    fa_ref[6:8] = jnp.zeros((2, width, channels), BF16)
    rows = fa_ref[...].reshape(8 * width, channels)

    for side, ref in enumerate((own_ref, mate_ref)):
        product = lax.dot_general(
            ref[0:half].reshape(half * width, channels),
            rows,
            (((1,), (1,)), ((), ())),
            preferred_element_type=F32,
        )
        for g in range(half):
            ib = index ^ (offsets[g] ^ side)
            start = (ib % 2) * 8 + ib // 2
            block = product[g * width : (g + 1) * width] * channels ** (-0.5)
            for c in range(2):
                vf_ref[c, pl.ds(start, width, stride=16), :] = block[
                    :, 128 * c : 128 * c + 128
                ]
    for c in range(4):
        vp_ref[:, 128 * c : 128 * c + 128] = vf_ref[c % 2].astype(BF16)

    def spread(k):
        s_ref[k % 2] = jnp.dot(vp_ref[...], at1_ref[k], preferred_element_type=F32)

    def hide(k):
        for net in range(2):
            weights = [w1_ref[2 * k + net, n : n + 1] for n in range(12)]
            bias = w1_ref[2 * k + net, 12:13]

            def load(r):
                return s_ref[k % 2, 8 * r : 8 * r + 8, 128 * net : 128 * net + 128]

            def emit(jb, sums):
                sums[1] = sums[1] + bias
                h_ref[k % 2, 16 * jb : 16 * jb + 16, 128 * net : 128 * net + 128] = jnp.maximum(
                    pair_of(sums).astype(BF16), 0
                )

            yield from b_taps(load, weights, emit, width)

    def gather_rows(k):
        both = jnp.dot(h_ref[k % 2], at2_ref[k], preferred_element_type=F32)
        t_ref[k % 2] = both[:, 0:128] + both[:, 128:256]

    def gather_taps(k):
        weights = [w2_ref[k, n : n + 1] for n in range(12)]

        def load(r):
            return t_ref[k % 2, 8 * r : 8 * r + 8, :]

        def emit(jb, sums):
            if k > 0:
                sums = [acc_ref[part, 8 * jb : 8 * jb + 8, :] + sums[part] for part in range(4)]
            if k < 7:
                for part in range(4):
                    acc_ref[part, 8 * jb : 8 * jb + 8, :] = sums[part]
            else:
                total = jnp.maximum(pair_of(sums) + bias2_ref[0], 0.0)
                nat_ref[pl.ds(jb, 8, stride=2 * width), :] = total[0:8]
                nat_ref[pl.ds(width + jb, 8, stride=2 * width), :] = total[8:16]

        yield from b_taps(load, weights, emit, width)

    for step in range(11):
        if step < 8:
            spread(step)
        if 2 <= step < 10:
            gather_rows(step - 2)
        ones = hide(step - 1) if 1 <= step < 9 else iter(())
        twos = gather_taps(step - 3) if step >= 3 else iter(())
        for _ in range(width):
            next(ones, None)
            next(twos, None)
            next(ones, None)

    turned = jnp.transpose(nat_ref[...], (1, 0))
    score = turned[0:64] + turned[64:128]
    best_ref[...] = jnp.max(score, axis=0, keepdims=True)
    best_b = jnp.max(score, axis=1, keepdims=True)
    score_ref[...] = score
    part_ref[...] = score * (score / (best_b + EPSILON))


def consensus(bias_second, weights, own, mate, outer, offsets, width):
    half = len(offsets)
    cells = 2 * half * width
    channels = own.shape[2]
    vmem = pl.BlockSpec(memory_space=pltpu.VMEM)
    return pl.pallas_call(
        functools.partial(consensus_kernel, offsets, width),
        out_shape=(
            jax.ShapeDtypeStruct((2 * width, cells), F32),
            jax.ShapeDtypeStruct((2 * width, cells), F32),
            jax.ShapeDtypeStruct((1, cells), F32),
        ),
        in_specs=[pl.BlockSpec(memory_space=pltpu.SMEM)] + [vmem] * 7,
        out_specs=(vmem, vmem, vmem),
        scratch_shapes=[
            pltpu.VMEM((8, width, channels), BF16),
            pltpu.VMEM((2, cells, 128), F32),
            pltpu.VMEM((cells, 512), BF16),
            pltpu.VMEM((2, cells, 256), F32),
            pltpu.VMEM((2, cells, 256), BF16),
            pltpu.VMEM((2, cells, 128), F32),
            pltpu.VMEM((4, cells // 2, 128), F32),
            pltpu.VMEM((cells, 128), F32),
        ],
        compiler_params=pltpu.CompilerParams(vmem_limit_bytes=32 << 20),
        cost_estimate=pl.CostEstimate(
            flops=2_000_000_000, bytes_accessed=4_500_000, transcendentals=0
        ),
    )(bias_second, *weights, own, mate, outer)


def exchange(value, mask, count):
    return lax.ppermute(value, "arow", [(i, i ^ mask) for i in range(count)])


def outer_pairs(groups, count):
    pairs = []
    for g in range(groups):
        for i in range(count):
            j = i + 1 if i % 2 else i - 1
            if 0 <= j < count:
                pairs.append((g * count + i, g * count + j))
            else:
                other = g ^ 1 if (g ^ 1) < groups else g
                pairs.append((g * count + i, other * count + i))
    return pairs


def fast(feat_a, feat_b, a_first, b_first, bias_first, a_second, b_second, bias_second):
    count = lax.axis_size("arow")
    groups = lax.axis_size("groups")
    width = feat_b.shape[1]
    masks = [(1 << b) | 1 for b in reversed(range(1, count.bit_length() - 1))]

    rows = feat_a.shape[0]
    near = lax.optimization_barrier(jnp.concatenate([feat_a, feat_b], axis=0))
    near_a, near_b = near[:rows], near[rows:]
    packed = pack(bias_first, a_first, b_first, a_second, b_second)
    held, offsets = feat_b, [0]
    for n, mask in enumerate(masks):
        if n == 1:
            feat_a, held, packed = lax.optimization_barrier((feat_a, held, packed))
            outer = lax.ppermute(feat_a, ("groups", "arow"), outer_pairs(groups, count))
        if n == 2:
            packed, outer = lax.optimization_barrier((packed, outer))
            weights = prepare(packed, width)
        received = exchange(held, mask, count)
        held = jnp.concatenate([near_b if n == 0 else held, received], axis=0)
        offsets = offsets + [o ^ mask for o in offsets]
    held, outer, weights, bias_second = lax.optimization_barrier(
        (held, outer, weights, bias_second)
    )
    own = jnp.concatenate([held, near_a], axis=0)
    mate = exchange(own, 1, count)

    score, part, best = consensus(bias_second, weights, own, mate, outer, offsets, width)
    for mask in masks + [1]:
        best = jnp.maximum(best, exchange(best, mask, count))
    out = part * (score / (best + EPSILON))
    return out.reshape(feat_a.shape[0], width, -1)


def on_device(feat_a, feat_b, *filters):
    count = lax.axis_size("arow")
    fits = (
        feat_a.shape == (2, 32, 256)
        and feat_b.shape == (1, 32, 256)
        and count == 16
        and filters[0].shape[0] == 8
    )
    return (fast if fits else general)(feat_a, feat_b, *filters)


def solution(mesh):
    return jax.shard_map(
        on_device,
        mesh=mesh,
        in_specs=(
            P(("groups", "arow"), None, None),
            P(("groups", "arow"), None, None),
            P(),
            P(),
            P(),
            P(),
            P(),
            P(),
        ),
        out_specs=P(("groups", "arow"), None, None),
        check_vma=False,
    )
```

```python
import functools

import jax
import jax.numpy as jnp
from jax import lax
from jax.experimental import pallas as pl
from jax.experimental.pallas import tpu as pltpu
from jax.sharding import PartitionSpec as P

EPSILON = 1e-05
F32 = jnp.float32
BF16 = jnp.bfloat16


def padded(cells, sides, width):
    for axis, dim in sides:
        count = lax.axis_size(axis)
        ends = count - 1
        head = lax.slice_in_dim(cells, 0, width, axis=dim)
        tail = lax.slice_in_dim(cells, cells.shape[dim] - width, cells.shape[dim], axis=dim)
        cells = jnp.concatenate(
            [
                lax.ppermute(tail, axis, [(i, (i + 1) % count) for i in range(ends)]),
                cells,
                lax.ppermute(head, axis, [((i + 1) % count, i) for i in range(ends)]),
            ],
            axis=dim,
        )
    return cells


def shifted_zero(values, along, offset):
    extent = values.shape[along]
    if offset == 0:
        return values
    widths = [(0, 0)] * values.ndim
    if offset > 0:
        widths[along] = (0, offset)
        return lax.slice_in_dim(jnp.pad(values, widths), offset, offset + extent, axis=along)
    widths[along] = (-offset, 0)
    return lax.slice_in_dim(jnp.pad(values, widths), 0, extent, axis=along)


def conv_a(values, kernel):
    out_rows = values.shape[-3] - 2
    result = 0.0
    for row_tap in range(3):
        row_slab = lax.slice_in_dim(
            values, row_tap, row_tap + out_rows, axis=values.ndim - 3
        ).astype(F32)
        for col_tap in range(3):
            result = result + kernel[..., row_tap, col_tap][..., None, None, None] * shifted_zero(
                row_slab, values.ndim - 2, col_tap - 1
            )
    return result


def conv_b(values, kernel, map_width):
    flat_pos = lax.broadcasted_iota(jnp.int32, (values.shape[-1],), 0) % map_width
    result = 0.0
    for row_tap in range(3):
        for col_tap in range(3):
            shifted = shifted_zero(
                values, values.ndim - 1, (row_tap - 1) * map_width + (col_tap - 1)
            )
            inside = ((flat_pos + col_tap - 1 >= 0) & (flat_pos + col_tap - 1 < map_width)).astype(
                F32
            )
            result = result + kernel[..., row_tap, col_tap][..., None, None, None] * (
                shifted * inside
            )
    return result


def first_layer(correlation, kern_a, kern_b, bias_one, map_width):
    spread = conv_a(correlation, kern_a)
    return jax.nn.relu(conv_b(spread, kern_b, map_width) + bias_one[:, None, None, None]).astype(
        BF16
    )


def second_layer(hidden, kern_a, kern_b, bias_two, map_width):
    spread = conv_a(hidden, kern_a)
    summed = jnp.sum(conv_b(spread, kern_b, map_width), axis=0)
    return jax.nn.relu(summed + bias_two[0])


def general(feat_a, feat_b, a_first, b_first, bias_first, a_second, b_second, bias_second):
    map_width = feat_b.shape[1]
    channels = feat_a.shape[2]
    b_cells = feat_b.shape[0] * lax.axis_size("arow") * map_width
    a_rows = feat_a.reshape(-1, channels)
    tile_product = lax.dot_general(
        a_rows,
        lax.all_gather(feat_b, "arow", axis=0, tiled=True).reshape(-1, channels),
        (((1,), (1,)), ((), ())),
        preferred_element_type=F32,
    )
    correlation = (
        (tile_product * channels ** (-0.5))
        .astype(BF16)
        .reshape(feat_a.shape[0], map_width, b_cells)
    )
    correlation = padded(correlation, (("arow", 0),), 1)

    def network(kern_a1, kern_b1, kern_a2, kern_b2):
        hidden = first_layer(correlation, kern_a1, kern_b1, bias_first, map_width)
        hidden = padded(hidden, (("arow", 1),), 1)
        return second_layer(hidden, kern_a2, kern_b2, bias_second, map_width)

    score = network(a_first, b_first, a_second, b_second)
    score = score + network(b_first, a_first, b_second, a_second)
    best_over_a = lax.pmax(jnp.max(score, axis=(0, 1)), "arow")
    best_over_b = jnp.max(score, axis=2)[..., None]
    return score * (score / (best_over_a + EPSILON)) * (score / (best_over_b + EPSILON))


def lane(shape):
    return lax.broadcasted_iota(jnp.int32, shape, 1)


def sublane(shape):
    return lax.broadcasted_iota(jnp.int32, shape, 0)


def two_terms(value):
    high = value.astype(BF16)
    return high, (value - high.astype(F32)).astype(BF16)


def first_weights(taps, at_ref, k, width, diag, row_is):
    for net in range(2):
        lanes = slice(128 * net, 128 * net + 128)
        for cr in range(6):
            block = jnp.zeros((width, 128), F32)
            for w in range(3):
                per_lane = jnp.zeros((1, 128), F32)
                for u in range(3):
                    if 0 <= cr - u <= 3:
                        per_lane = jnp.where(row_is[cr - u], taps[net][3 * u + w], per_lane)
                block = jnp.where(diag[w], per_lane, block)
            high, low = two_terms(block)
            at_ref[k, cr * width : (cr + 1) * width, lanes] = high
            at_ref[k, (8 + cr) * width : (9 + cr) * width, lanes] = low
        for base in (6, 14):
            at_ref[k, base * width : (base + 2) * width, lanes] = jnp.zeros((2 * width, 128), BF16)


def second_weights(taps, at_ref, k, width, keep, diag, row_is):
    for net in range(2):
        for hr in range(4):
            block = jnp.zeros((width, 128), F32)
            for w in range(3):
                per_lane = jnp.zeros((1, 128), F32)
                for u in range(3):
                    if 0 <= hr - u <= 1:
                        per_lane = jnp.where(
                            row_is[2 * net + hr - u], taps[net][3 * u + w], per_lane
                        )
                if hr in keep:
                    per_lane = per_lane * keep[hr]
                block = jnp.where(diag[w], per_lane, block)
            high, low = two_terms(block)
            rows = slice((4 * net + hr) * width, (4 * net + hr + 1) * width)
            at_ref[k, rows, 0:128] = high
            at_ref[k, rows, 128:256] = low


def minimal_filter(taps):
    parts = [[], [], [], []]
    for t in range(3):
        ends = 0.5 * (taps[t] + taps[6 + t])
        middle = 0.5 * taps[3 + t]
        for part, row in zip(parts, (taps[t], ends + middle, ends - middle, taps[6 + t])):
            part.append(row)
    return sum(parts, [])


def b_taps(load, weights, emit, width):
    top = sublane((8, 128)) == 0
    bottom = sublane((8, 128)) == 7

    def column(jb):
        even, odd = load(2 * jb), load(2 * jb + 1)
        above = jnp.where(top, 0.0, pltpu.roll(odd, 1, 0))
        below = jnp.where(bottom, 0.0, pltpu.roll(even, 7, 0))
        return above - odd, even + odd, odd - even, even - below

    window = [None, column(0), column(1)]
    for jb in range(width):
        sums = []
        for part in range(4):
            total = None
            for t in range(3):
                if window[t] is None:
                    continue
                term = weights[3 * part + t] * window[t][part]
                total = term if total is None else total + term
            sums.append(total)
        emit(jb, sums)
        yield
        window = [window[1], window[2], column(jb + 2) if jb + 2 < width else None]


def pair_of(sums):
    first, second, third, fourth = sums
    return jnp.concatenate([first + second + third, second - third - fourth], axis=0)


def prepare_kernel(width, packed_ref, at1_ref, at2_ref, w1_ref, w2_ref):
    index = lax.axis_index("arow")
    keep = {
        0: (index != 0).astype(F32),
        3: (index != lax.axis_size("arow") - 1).astype(F32),
    }

    half_lanes = lane((1, 128)) < 64
    col = lane((width, 128)) % width
    diag = [sublane((width, 128)) + 1 - col == w for w in range(3)]
    row_is = [lane((1, 128)) // width == r for r in range(4)]
    for k in range(8):
        banks = [
            [jnp.full((1, 128), packed_ref[3 * n + tap // 3, tap % 3, k], F32) for tap in range(9)]
            for n in range(4)
        ]
        first, second = banks[0:2], banks[2:4]
        first_weights(first, at1_ref, k, width, diag, row_is)
        second_weights(second, at2_ref, k, width, keep, diag, row_is)
        for net in range(2):
            for n, row in enumerate(minimal_filter(first[1 - net])):
                w1_ref[2 * k + net, n : n + 1] = row
            w1_ref[2 * k + net, 12:13] = jnp.full((1, 128), packed_ref[12, 0, k], F32)
        mixed = [jnp.where(half_lanes, second[1][tap], second[0][tap]) for tap in range(9)]
        for n, row in enumerate(minimal_filter(mixed)):
            w2_ref[k, n : n + 1] = row


def pack(bias, *banks):
    packed = jnp.pad(bias.reshape(1, 1, 8), ((12, 0), (0, 2), (0, 0)))
    for n, f in enumerate(banks):
        packed += jnp.pad(f.transpose(1, 2, 0), ((3 * n, 10 - 3 * n), (0, 0), (0, 0)))
    return packed


def prepare(packed, width):
    vmem = pl.BlockSpec(memory_space=pltpu.VMEM)
    return pl.pallas_call(
        functools.partial(prepare_kernel, width),
        out_shape=(
            jax.ShapeDtypeStruct((8, 512, 256), BF16),
            jax.ShapeDtypeStruct((8, 256, 256), BF16),
            jax.ShapeDtypeStruct((16, 16, 128), F32),
            jax.ShapeDtypeStruct((8, 16, 128), F32),
        ),
        in_specs=[pl.BlockSpec(memory_space=pltpu.SMEM)],
        out_specs=(vmem,) * 4,
        compiler_params=pltpu.CompilerParams(vmem_limit_bytes=16 << 20),
        cost_estimate=pl.CostEstimate(
            flops=2_000_000_000, bytes_accessed=3_500_000, transcendentals=0
        ),
    )(packed)


def consensus_kernel(
    offsets,
    width,
    bias2_ref,
    at1_ref,
    at2_ref,
    w1_ref,
    w2_ref,
    own_ref,
    mate_ref,
    outer_ref,
    score_ref,
    best_ref,
    fa_ref,
    vf_ref,
    vp_ref,
    s_ref,
    h_ref,
    t_ref,
    acc_ref,
    nat_ref,
):
    half = len(offsets)
    channels = own_ref.shape[2]
    index = lax.axis_index("arow")
    parity = index % 2
    inside = jnp.logical_and(index != 0, index != lax.axis_size("arow") - 1)

    fa_ref[2:4] = own_ref[half : half + 2]
    fa_ref[pl.ds(4 - 4 * parity, 2)] = mate_ref[half : half + 2]
    fa_ref[pl.ds(4 * parity, 2)] = outer_ref[...] * inside.astype(BF16)
    fa_ref[6:8] = jnp.zeros((2, width, channels), BF16)
    rows = fa_ref[...].reshape(8 * width, channels)

    for side, ref in enumerate((own_ref, mate_ref)):
        product = lax.dot_general(
            ref[0:half].reshape(half * width, channels),
            rows,
            (((1,), (1,)), ((), ())),
            preferred_element_type=F32,
        )
        for g in range(half):
            ib = index ^ (offsets[g] ^ side)
            start = (ib % 2) * 8 + ib // 2
            block = product[g * width : (g + 1) * width] * channels ** (-0.5)
            for c in range(2):
                vf_ref[c, pl.ds(start, width, stride=16), :] = block[
                    :, 128 * c : 128 * c + 128
                ]
    for c in range(4):
        vp_ref[:, 128 * c : 128 * c + 128] = vf_ref[c % 2].astype(BF16)

    def spread(k):
        s_ref[k % 2] = jnp.dot(vp_ref[...], at1_ref[k], preferred_element_type=F32)

    def hide(k):
        for net in range(2):
            weights = [w1_ref[2 * k + net, n : n + 1] for n in range(12)]
            bias = w1_ref[2 * k + net, 12:13]

            def load(r):
                return s_ref[k % 2, 8 * r : 8 * r + 8, 128 * net : 128 * net + 128]

            def emit(jb, sums):
                sums[1] = sums[1] + bias
                h_ref[k % 2, 16 * jb : 16 * jb + 16, 128 * net : 128 * net + 128] = jnp.maximum(
                    pair_of(sums).astype(BF16), 0
                )

            yield from b_taps(load, weights, emit, width)

    def gather_rows(k):
        both = jnp.dot(h_ref[k % 2], at2_ref[k], preferred_element_type=F32)
        t_ref[k % 2] = both[:, 0:128] + both[:, 128:256]

    def gather_taps(k):
        weights = [w2_ref[k, n : n + 1] for n in range(12)]

        def load(r):
            return t_ref[k % 2, 8 * r : 8 * r + 8, :]

        def emit(jb, sums):
            if k > 0:
                sums = [acc_ref[part, 8 * jb : 8 * jb + 8, :] + sums[part] for part in range(4)]
            if k < 7:
                for part in range(4):
                    acc_ref[part, 8 * jb : 8 * jb + 8, :] = sums[part]
            else:
                total = jnp.maximum(pair_of(sums) + bias2_ref[0], 0.0)
                nat_ref[pl.ds(jb, 8, stride=2 * width), :] = total[0:8]
                nat_ref[pl.ds(width + jb, 8, stride=2 * width), :] = total[8:16]

        yield from b_taps(load, weights, emit, width)

    for step in range(11):
        if step < 8:
            spread(step)
        if 2 <= step < 10:
            gather_rows(step - 2)
        ones = hide(step - 1) if 1 <= step < 9 else iter(())
        twos = gather_taps(step - 3) if step >= 3 else iter(())
        for _ in range(width):
            next(ones, None)
            next(twos, None)
            next(ones, None)

    turned = jnp.transpose(nat_ref[...], (1, 0))
    score = turned[0:64] + turned[64:128]
    best_ref[...] = jnp.max(score, axis=0, keepdims=True)
    score_ref[...] = score


def consensus(bias_second, weights, own, mate, outer, offsets, width):
    half = len(offsets)
    cells = 2 * half * width
    channels = own.shape[2]
    vmem = pl.BlockSpec(memory_space=pltpu.VMEM)
    return pl.pallas_call(
        functools.partial(consensus_kernel, offsets, width),
        out_shape=(
            jax.ShapeDtypeStruct((2 * width, cells), F32),
            jax.ShapeDtypeStruct((1, cells), F32),
        ),
        in_specs=[pl.BlockSpec(memory_space=pltpu.SMEM)] + [vmem] * 7,
        out_specs=(vmem, vmem),
        scratch_shapes=[
            pltpu.VMEM((8, width, channels), BF16),
            pltpu.VMEM((2, cells, 128), F32),
            pltpu.VMEM((cells, 512), BF16),
            pltpu.VMEM((2, cells, 256), F32),
            pltpu.VMEM((2, cells, 256), BF16),
            pltpu.VMEM((2, cells, 128), F32),
            pltpu.VMEM((4, cells // 2, 128), F32),
            pltpu.VMEM((cells, 128), F32),
        ],
        compiler_params=pltpu.CompilerParams(vmem_limit_bytes=32 << 20),
        cost_estimate=pl.CostEstimate(
            flops=2_000_000_000, bytes_accessed=4_500_000, transcendentals=0
        ),
    )(bias_second, *weights, own, mate, outer)


def exchange(value, mask, count):
    return lax.ppermute(value, "arow", [(i, i ^ mask) for i in range(count)])


def outer_pairs(groups, count):
    pairs = []
    for g in range(groups):
        for i in range(count):
            j = i + 1 if i % 2 else i - 1
            if 0 <= j < count:
                pairs.append((g * count + i, g * count + j))
            else:
                other = g ^ 1 if (g ^ 1) < groups else g
                pairs.append((g * count + i, other * count + i))
    return pairs


def fast(feat_a, feat_b, a_first, b_first, bias_first, a_second, b_second, bias_second):
    count = lax.axis_size("arow")
    groups = lax.axis_size("groups")
    width = feat_b.shape[1]
    masks = [(1 << b) | 1 for b in reversed(range(1, count.bit_length() - 1))]

    rows = feat_a.shape[0]
    near = lax.optimization_barrier(jnp.concatenate([feat_a, feat_b], axis=0))
    near_a, near_b = near[:rows], near[rows:]
    packed = pack(bias_first, a_first, b_first, a_second, b_second)
    held, offsets = feat_b, [0]
    for n, mask in enumerate(masks):
        if n == 1:
            feat_a, held, packed = lax.optimization_barrier((feat_a, held, packed))
            outer = lax.ppermute(feat_a, ("groups", "arow"), outer_pairs(groups, count))
        if n == 2:
            packed, held = lax.optimization_barrier((packed, held))
            weights = prepare(packed, width)
        received = exchange(held, mask, count)
        held = jnp.concatenate([near_b if n == 0 else held, received], axis=0)
        offsets = offsets + [o ^ mask for o in offsets]
    held, outer, weights, bias_second = lax.optimization_barrier(
        (held, outer, weights, bias_second)
    )
    own = jnp.concatenate([held, near_a], axis=0)
    mate = exchange(own, 1, count)

    score, best = consensus(bias_second, weights, own, mate, outer, offsets, width)
    part = lax.optimization_barrier(
        score * (score / (jnp.max(score, axis=1, keepdims=True) + EPSILON))
    )
    for mask in masks + [1]:
        best = jnp.maximum(best, exchange(best, mask, count))
    out = part * (score / (best + EPSILON))
    return out.reshape(feat_a.shape[0], width, -1)


def on_device(feat_a, feat_b, *filters):
    count = lax.axis_size("arow")
    fits = (
        feat_a.shape == (2, 32, 256)
        and feat_b.shape == (1, 32, 256)
        and count == 16
        and filters[0].shape[0] == 8
    )
    return (fast if fits else general)(feat_a, feat_b, *filters)


def solution(mesh):
    return jax.shard_map(
        on_device,
        mesh=mesh,
        in_specs=(
            P(("groups", "arow"), None, None),
            P(("groups", "arow"), None, None),
            P(),
            P(),
            P(),
            P(),
            P(),
            P(),
        ),
        out_specs=P(("groups", "arow"), None, None),
        check_vma=False,
    )
```

```python
import functools

import jax
import jax.numpy as jnp
from jax import lax
from jax.experimental import pallas as pl
from jax.experimental.pallas import tpu as pltpu
from jax.sharding import PartitionSpec as P

EPSILON = 1e-05
F32 = jnp.float32
BF16 = jnp.bfloat16


def padded(cells, sides, width):
    for axis, dim in sides:
        count = lax.axis_size(axis)
        ends = count - 1
        head = lax.slice_in_dim(cells, 0, width, axis=dim)
        tail = lax.slice_in_dim(cells, cells.shape[dim] - width, cells.shape[dim], axis=dim)
        cells = jnp.concatenate(
            [
                lax.ppermute(tail, axis, [(i, (i + 1) % count) for i in range(ends)]),
                cells,
                lax.ppermute(head, axis, [((i + 1) % count, i) for i in range(ends)]),
            ],
            axis=dim,
        )
    return cells


def shifted_zero(values, along, offset):
    extent = values.shape[along]
    if offset == 0:
        return values
    widths = [(0, 0)] * values.ndim
    if offset > 0:
        widths[along] = (0, offset)
        return lax.slice_in_dim(jnp.pad(values, widths), offset, offset + extent, axis=along)
    widths[along] = (-offset, 0)
    return lax.slice_in_dim(jnp.pad(values, widths), 0, extent, axis=along)


def conv_a(values, kernel):
    out_rows = values.shape[-3] - 2
    result = 0.0
    for row_tap in range(3):
        row_slab = lax.slice_in_dim(
            values, row_tap, row_tap + out_rows, axis=values.ndim - 3
        ).astype(F32)
        for col_tap in range(3):
            result = result + kernel[..., row_tap, col_tap][..., None, None, None] * shifted_zero(
                row_slab, values.ndim - 2, col_tap - 1
            )
    return result


def conv_b(values, kernel, map_width):
    flat_pos = lax.broadcasted_iota(jnp.int32, (values.shape[-1],), 0) % map_width
    result = 0.0
    for row_tap in range(3):
        for col_tap in range(3):
            shifted = shifted_zero(
                values, values.ndim - 1, (row_tap - 1) * map_width + (col_tap - 1)
            )
            inside = ((flat_pos + col_tap - 1 >= 0) & (flat_pos + col_tap - 1 < map_width)).astype(
                F32
            )
            result = result + kernel[..., row_tap, col_tap][..., None, None, None] * (
                shifted * inside
            )
    return result


def first_layer(correlation, kern_a, kern_b, bias_one, map_width):
    spread = conv_a(correlation, kern_a)
    return jax.nn.relu(conv_b(spread, kern_b, map_width) + bias_one[:, None, None, None]).astype(
        BF16
    )


def second_layer(hidden, kern_a, kern_b, bias_two, map_width):
    spread = conv_a(hidden, kern_a)
    summed = jnp.sum(conv_b(spread, kern_b, map_width), axis=0)
    return jax.nn.relu(summed + bias_two[0])


def general(feat_a, feat_b, a_first, b_first, bias_first, a_second, b_second, bias_second):
    map_width = feat_b.shape[1]
    channels = feat_a.shape[2]
    b_cells = feat_b.shape[0] * lax.axis_size("arow") * map_width
    a_rows = feat_a.reshape(-1, channels)
    tile_product = lax.dot_general(
        a_rows,
        lax.all_gather(feat_b, "arow", axis=0, tiled=True).reshape(-1, channels),
        (((1,), (1,)), ((), ())),
        preferred_element_type=F32,
    )
    correlation = (
        (tile_product * channels ** (-0.5))
        .astype(BF16)
        .reshape(feat_a.shape[0], map_width, b_cells)
    )
    correlation = padded(correlation, (("arow", 0),), 1)

    def network(kern_a1, kern_b1, kern_a2, kern_b2):
        hidden = first_layer(correlation, kern_a1, kern_b1, bias_first, map_width)
        hidden = padded(hidden, (("arow", 1),), 1)
        return second_layer(hidden, kern_a2, kern_b2, bias_second, map_width)

    score = network(a_first, b_first, a_second, b_second)
    score = score + network(b_first, a_first, b_second, a_second)
    best_over_a = lax.pmax(jnp.max(score, axis=(0, 1)), "arow")
    best_over_b = jnp.max(score, axis=2)[..., None]
    return score * (score / (best_over_a + EPSILON)) * (score / (best_over_b + EPSILON))


def lane(shape):
    return lax.broadcasted_iota(jnp.int32, shape, 1)


def sublane(shape):
    return lax.broadcasted_iota(jnp.int32, shape, 0)


def two_terms(value):
    high = value.astype(BF16)
    return high, (value - high.astype(F32)).astype(BF16)


def first_weights(taps, at_ref, k, width, diag, row_is):
    for net in range(2):
        lanes = slice(128 * net, 128 * net + 128)
        for cr in range(6):
            block = jnp.zeros((width, 128), F32)
            for w in range(3):
                per_lane = jnp.zeros((1, 128), F32)
                for u in range(3):
                    if 0 <= cr - u <= 3:
                        per_lane = jnp.where(row_is[cr - u], taps[net][3 * u + w], per_lane)
                block = jnp.where(diag[w], per_lane, block)
            high, low = two_terms(block)
            at_ref[k, cr * width : (cr + 1) * width, lanes] = high
            at_ref[k, (8 + cr) * width : (9 + cr) * width, lanes] = low
        for base in (6, 14):
            at_ref[k, base * width : (base + 2) * width, lanes] = jnp.zeros((2 * width, 128), BF16)


def second_weights(taps, at_ref, k, width, keep, diag, row_is):
    for net in range(2):
        for hr in range(4):
            block = jnp.zeros((width, 128), F32)
            for w in range(3):
                per_lane = jnp.zeros((1, 128), F32)
                for u in range(3):
                    if 0 <= hr - u <= 1:
                        per_lane = jnp.where(
                            row_is[2 * net + hr - u], taps[net][3 * u + w], per_lane
                        )
                if hr in keep:
                    per_lane = per_lane * keep[hr]
                block = jnp.where(diag[w], per_lane, block)
            high, low = two_terms(block)
            rows = slice((4 * net + hr) * width, (4 * net + hr + 1) * width)
            at_ref[k, rows, 0:128] = high
            at_ref[k, rows, 128:256] = low


def minimal_filter(taps):
    parts = [[], [], [], []]
    for t in range(3):
        ends = 0.5 * (taps[t] + taps[6 + t])
        middle = 0.5 * taps[3 + t]
        for part, row in zip(parts, (taps[t], ends + middle, ends - middle, taps[6 + t])):
            part.append(row)
    return sum(parts, [])


def b_taps(load, weights, emit, width):
    top = sublane((8, 128)) == 0
    bottom = sublane((8, 128)) == 7

    def column(jb):
        even, odd = load(2 * jb), load(2 * jb + 1)
        above = jnp.where(top, 0.0, pltpu.roll(odd, 1, 0))
        below = jnp.where(bottom, 0.0, pltpu.roll(even, 7, 0))
        return above - odd, even + odd, odd - even, even - below

    window = [None, column(0), column(1)]
    for jb in range(width):
        sums = []
        for part in range(4):
            total = None
            for t in range(3):
                if window[t] is None:
                    continue
                term = weights[3 * part + t] * window[t][part]
                total = term if total is None else total + term
            sums.append(total)
        emit(jb, sums)
        yield
        window = [window[1], window[2], column(jb + 2) if jb + 2 < width else None]


def pair_of(sums):
    first, second, third, fourth = sums
    return jnp.concatenate([first + second + third, second - third - fourth], axis=0)


def prepare_kernel(width, packed_ref, at1_ref, at2_ref, w1_ref, w2_ref):
    index = lax.axis_index("arow")
    keep = {
        0: (index != 0).astype(F32),
        3: (index != lax.axis_size("arow") - 1).astype(F32),
    }

    half_lanes = lane((1, 128)) < 64
    col = lane((width, 128)) % width
    diag = [sublane((width, 128)) + 1 - col == w for w in range(3)]
    row_is = [lane((1, 128)) // width == r for r in range(4)]
    for k in range(8):
        banks = [
            [jnp.full((1, 128), packed_ref[3 * n + tap // 3, tap % 3, k], F32) for tap in range(9)]
            for n in range(4)
        ]
        first, second = banks[0:2], banks[2:4]
        first_weights(first, at1_ref, k, width, diag, row_is)
        second_weights(second, at2_ref, k, width, keep, diag, row_is)
        for net in range(2):
            for n, row in enumerate(minimal_filter(first[1 - net])):
                w1_ref[2 * k + net, n : n + 1] = row
            w1_ref[2 * k + net, 12:13] = jnp.full((1, 128), packed_ref[12, 0, k], F32)
        mixed = [jnp.where(half_lanes, second[1][tap], second[0][tap]) for tap in range(9)]
        for n, row in enumerate(minimal_filter(mixed)):
            w2_ref[k, n : n + 1] = row


def pack(bias, *banks):
    packed = jnp.pad(bias.reshape(1, 1, 8), ((12, 0), (0, 2), (0, 0)))
    for n, f in enumerate(banks):
        packed += jnp.pad(f.transpose(1, 2, 0), ((3 * n, 10 - 3 * n), (0, 0), (0, 0)))
    return packed


def prepare(packed, width):
    vmem = pl.BlockSpec(memory_space=pltpu.VMEM)
    return pl.pallas_call(
        functools.partial(prepare_kernel, width),
        out_shape=(
            jax.ShapeDtypeStruct((8, 512, 256), BF16),
            jax.ShapeDtypeStruct((8, 256, 256), BF16),
            jax.ShapeDtypeStruct((16, 16, 128), F32),
            jax.ShapeDtypeStruct((8, 16, 128), F32),
        ),
        in_specs=[pl.BlockSpec(memory_space=pltpu.SMEM)],
        out_specs=(vmem,) * 4,
        compiler_params=pltpu.CompilerParams(vmem_limit_bytes=16 << 20),
        cost_estimate=pl.CostEstimate(
            flops=2_000_000_000, bytes_accessed=3_500_000, transcendentals=0
        ),
    )(packed)


def consensus_kernel(
    offsets,
    width,
    bias2_ref,
    at1_ref,
    at2_ref,
    w1_ref,
    w2_ref,
    own_ref,
    mate_ref,
    outer_ref,
    score_ref,
    best_ref,
    fa_ref,
    vf_ref,
    vp_ref,
    s_ref,
    h_ref,
    t_ref,
    acc_ref,
    nat_ref,
):
    half = len(offsets)
    channels = own_ref.shape[2]
    index = lax.axis_index("arow")
    parity = index % 2
    inside = jnp.logical_and(index != 0, index != lax.axis_size("arow") - 1)

    fa_ref[2:4] = own_ref[half : half + 2]
    fa_ref[pl.ds(4 - 4 * parity, 2)] = mate_ref[half : half + 2]
    fa_ref[pl.ds(4 * parity, 2)] = outer_ref[...] * inside.astype(BF16)
    fa_ref[6:8] = jnp.zeros((2, width, channels), BF16)
    rows = fa_ref[...].reshape(8 * width, channels)

    for side, ref in enumerate((own_ref, mate_ref)):
        product = lax.dot_general(
            ref[0:half].reshape(half * width, channels),
            rows,
            (((1,), (1,)), ((), ())),
            preferred_element_type=F32,
        )
        for g in range(half):
            ib = index ^ (offsets[g] ^ side)
            start = (ib % 2) * 8 + ib // 2
            block = product[g * width : (g + 1) * width] * channels ** (-0.5)
            for c in range(2):
                vf_ref[c, pl.ds(start, width, stride=16), :] = block[
                    :, 128 * c : 128 * c + 128
                ]
    for c in range(4):
        vp_ref[:, 128 * c : 128 * c + 128] = vf_ref[c % 2, 0 : 2 * half * width].astype(BF16)

    def spread(k):
        s_ref[k % 2] = jnp.dot(vp_ref[...], at1_ref[k], preferred_element_type=F32)

    def hide(k):
        for net in range(2):
            weights = [w1_ref[2 * k + net, n : n + 1] for n in range(12)]
            bias = w1_ref[2 * k + net, 12:13]

            def load(r):
                return s_ref[k % 2, 8 * r : 8 * r + 8, 128 * net : 128 * net + 128]

            def emit(jb, sums):
                sums[1] = sums[1] + bias
                h_ref[k % 2, 16 * jb : 16 * jb + 16, 128 * net : 128 * net + 128] = jnp.maximum(
                    pair_of(sums).astype(BF16), 0
                )

            yield from b_taps(load, weights, emit, width)

    def gather_rows(k):
        both = jnp.dot(h_ref[k % 2], at2_ref[k], preferred_element_type=F32)
        t_ref[k % 2] = both[:, 0:128] + both[:, 128:256]

    def gather_taps(k):
        weights = [w2_ref[k, n : n + 1] for n in range(12)]

        def load(r):
            return t_ref[k % 2, 8 * r : 8 * r + 8, :]

        def emit(jb, sums):
            if k > 0:
                sums = [acc_ref[part, 8 * jb : 8 * jb + 8, :] + sums[part] for part in range(4)]
            if k < 7:
                for part in range(4):
                    acc_ref[part, 8 * jb : 8 * jb + 8, :] = sums[part]
            else:
                total = jnp.maximum(pair_of(sums) + bias2_ref[0], 0.0)
                nat_ref[pl.ds(jb, 8, stride=2 * width), :] = total[0:8]
                nat_ref[pl.ds(width + jb, 8, stride=2 * width), :] = total[8:16]

        yield from b_taps(load, weights, emit, width)

    for step in range(11):
        if step < 8:
            spread(step)
        if 2 <= step < 10:
            gather_rows(step - 2)
        ones = hide(step - 1) if 1 <= step < 9 else iter(())
        twos = gather_taps(step - 3) if step >= 3 else iter(())
        for _ in range(width):
            next(ones, None)
            next(twos, None)
            next(ones, None)

    turned = jnp.transpose(nat_ref[0 : 2 * half * width], (1, 0))
    score = turned[0:64] + turned[64:128]
    best_ref[...] = jnp.max(score, axis=0, keepdims=True)
    score_ref[...] = score


def consensus(bias_second, weights, own, mate, outer, offsets, width):
    half = len(offsets)
    cells = 2 * half * width
    channels = own.shape[2]
    vmem = pl.BlockSpec(memory_space=pltpu.VMEM)
    return pl.pallas_call(
        functools.partial(consensus_kernel, offsets, width),
        out_shape=(
            jax.ShapeDtypeStruct((2 * width, cells), F32),
            jax.ShapeDtypeStruct((1, cells), F32),
        ),
        in_specs=[pl.BlockSpec(memory_space=pltpu.SMEM)] + [vmem] * 7,
        out_specs=(vmem, vmem),
        scratch_shapes=[
            pltpu.VMEM((8, width, channels), BF16),
            pltpu.VMEM((2, cells + 16, 128), F32),
            pltpu.VMEM((cells, 512), BF16),
            pltpu.VMEM((2, cells, 256), F32),
            pltpu.VMEM((2, cells, 256), BF16),
            pltpu.VMEM((2, cells, 128), F32),
            pltpu.VMEM((4, cells // 2, 128), F32),
            pltpu.VMEM((cells + 2 * width, 128), F32),
        ],
        compiler_params=pltpu.CompilerParams(vmem_limit_bytes=32 << 20),
        cost_estimate=pl.CostEstimate(
            flops=2_000_000_000, bytes_accessed=4_500_000, transcendentals=0
        ),
    )(bias_second, *weights, own, mate, outer)


def exchange(value, mask, count):
    return lax.ppermute(value, "arow", [(i, i ^ mask) for i in range(count)])


def outer_pairs(groups, count):
    pairs = []
    for g in range(groups):
        for i in range(count):
            j = i + 1 if i % 2 else i - 1
            if 0 <= j < count:
                pairs.append((g * count + i, g * count + j))
            else:
                other = g ^ 1 if (g ^ 1) < groups else g
                pairs.append((g * count + i, other * count + i))
    return pairs


def fast(feat_a, feat_b, a_first, b_first, bias_first, a_second, b_second, bias_second):
    count = lax.axis_size("arow")
    groups = lax.axis_size("groups")
    width = feat_b.shape[1]
    masks = [(1 << b) | 1 for b in reversed(range(1, count.bit_length() - 1))]

    rows = feat_a.shape[0]
    near = lax.optimization_barrier(jnp.concatenate([feat_a, feat_b], axis=0))
    near_a, near_b = near[:rows], near[rows:]
    packed = pack(bias_first, a_first, b_first, a_second, b_second)
    held, offsets = feat_b, [0]
    for n, mask in enumerate(masks):
        if n == 1:
            feat_a, held, packed = lax.optimization_barrier((feat_a, held, packed))
            outer = lax.ppermute(feat_a, ("groups", "arow"), outer_pairs(groups, count))
        if n == 2:
            packed, held = lax.optimization_barrier((packed, held))
            weights = prepare(packed, width)
        received = exchange(held, mask, count)
        held = jnp.concatenate([near_b if n == 0 else held, received], axis=0)
        offsets = offsets + [o ^ mask for o in offsets]
    held, outer, weights, bias_second = lax.optimization_barrier(
        (held, outer, weights, bias_second)
    )
    own = jnp.concatenate([held, near_a], axis=0)
    mate = exchange(own, 1, count)

    score, best = consensus(bias_second, weights, own, mate, outer, offsets, width)
    part = lax.optimization_barrier(
        score * (score / (jnp.max(score, axis=1, keepdims=True) + EPSILON))
    )
    for mask in masks + [1]:
        best = jnp.maximum(best, exchange(best, mask, count))
    out = part * (score / (best + EPSILON))
    return out.reshape(feat_a.shape[0], width, -1)


def on_device(feat_a, feat_b, *filters):
    count = lax.axis_size("arow")
    fits = (
        feat_a.shape == (2, 32, 256)
        and feat_b.shape == (1, 32, 256)
        and count == 16
        and filters[0].shape[0] == 8
    )
    return (fast if fits else general)(feat_a, feat_b, *filters)


def solution(mesh):
    return jax.shard_map(
        on_device,
        mesh=mesh,
        in_specs=(
            P(("groups", "arow"), None, None),
            P(("groups", "arow"), None, None),
            P(),
            P(),
            P(),
            P(),
            P(),
            P(),
        ),
        out_specs=P(("groups", "arow"), None, None),
        check_vma=False,
    )
```

```python
import functools

import jax
import jax.numpy as jnp
from jax import lax
from jax.experimental import pallas as pl
from jax.experimental.pallas import tpu as pltpu
from jax.sharding import PartitionSpec as P

EPSILON = 1e-05
F32 = jnp.float32
BF16 = jnp.bfloat16


def padded(cells, sides, width):
    for axis, dim in sides:
        count = lax.axis_size(axis)
        ends = count - 1
        head = lax.slice_in_dim(cells, 0, width, axis=dim)
        tail = lax.slice_in_dim(cells, cells.shape[dim] - width, cells.shape[dim], axis=dim)
        cells = jnp.concatenate(
            [
                lax.ppermute(tail, axis, [(i, (i + 1) % count) for i in range(ends)]),
                cells,
                lax.ppermute(head, axis, [((i + 1) % count, i) for i in range(ends)]),
            ],
            axis=dim,
        )
    return cells


def shifted_zero(values, along, offset):
    extent = values.shape[along]
    if offset == 0:
        return values
    widths = [(0, 0)] * values.ndim
    if offset > 0:
        widths[along] = (0, offset)
        return lax.slice_in_dim(jnp.pad(values, widths), offset, offset + extent, axis=along)
    widths[along] = (-offset, 0)
    return lax.slice_in_dim(jnp.pad(values, widths), 0, extent, axis=along)


def conv_a(values, kernel):
    out_rows = values.shape[-3] - 2
    result = 0.0
    for row_tap in range(3):
        row_slab = lax.slice_in_dim(
            values, row_tap, row_tap + out_rows, axis=values.ndim - 3
        ).astype(F32)
        for col_tap in range(3):
            result = result + kernel[..., row_tap, col_tap][..., None, None, None] * shifted_zero(
                row_slab, values.ndim - 2, col_tap - 1
            )
    return result


def conv_b(values, kernel, map_width):
    flat_pos = lax.broadcasted_iota(jnp.int32, (values.shape[-1],), 0) % map_width
    result = 0.0
    for row_tap in range(3):
        for col_tap in range(3):
            shifted = shifted_zero(
                values, values.ndim - 1, (row_tap - 1) * map_width + (col_tap - 1)
            )
            inside = ((flat_pos + col_tap - 1 >= 0) & (flat_pos + col_tap - 1 < map_width)).astype(
                F32
            )
            result = result + kernel[..., row_tap, col_tap][..., None, None, None] * (
                shifted * inside
            )
    return result


def first_layer(correlation, kern_a, kern_b, bias_one, map_width):
    spread = conv_a(correlation, kern_a)
    return jax.nn.relu(conv_b(spread, kern_b, map_width) + bias_one[:, None, None, None]).astype(
        BF16
    )


def second_layer(hidden, kern_a, kern_b, bias_two, map_width):
    spread = conv_a(hidden, kern_a)
    summed = jnp.sum(conv_b(spread, kern_b, map_width), axis=0)
    return jax.nn.relu(summed + bias_two[0])


def general(feat_a, feat_b, a_first, b_first, bias_first, a_second, b_second, bias_second):
    map_width = feat_b.shape[1]
    channels = feat_a.shape[2]
    b_cells = feat_b.shape[0] * lax.axis_size("arow") * map_width
    a_rows = feat_a.reshape(-1, channels)
    tile_product = lax.dot_general(
        a_rows,
        lax.all_gather(feat_b, "arow", axis=0, tiled=True).reshape(-1, channels),
        (((1,), (1,)), ((), ())),
        preferred_element_type=F32,
    )
    correlation = (
        (tile_product * channels ** (-0.5))
        .astype(BF16)
        .reshape(feat_a.shape[0], map_width, b_cells)
    )
    correlation = padded(correlation, (("arow", 0),), 1)

    def network(kern_a1, kern_b1, kern_a2, kern_b2):
        hidden = first_layer(correlation, kern_a1, kern_b1, bias_first, map_width)
        hidden = padded(hidden, (("arow", 1),), 1)
        return second_layer(hidden, kern_a2, kern_b2, bias_second, map_width)

    score = network(a_first, b_first, a_second, b_second)
    score = score + network(b_first, a_first, b_second, a_second)
    best_over_a = lax.pmax(jnp.max(score, axis=(0, 1)), "arow")
    best_over_b = jnp.max(score, axis=2)[..., None]
    return score * (score / (best_over_a + EPSILON)) * (score / (best_over_b + EPSILON))


def lane(shape):
    return lax.broadcasted_iota(jnp.int32, shape, 1)


def sublane(shape):
    return lax.broadcasted_iota(jnp.int32, shape, 0)


def two_terms(value):
    high = value.astype(BF16)
    return high, (value - high.astype(F32)).astype(BF16)


def first_weights(taps, at_ref, k, width, diag, row_is):
    for net in range(2):
        lanes = slice(128 * net, 128 * net + 128)
        for cr in range(6):
            block = jnp.zeros((width, 128), F32)
            for w in range(3):
                per_lane = jnp.zeros((1, 128), F32)
                for u in range(3):
                    if 0 <= cr - u <= 3:
                        per_lane = jnp.where(row_is[cr - u], taps[net][3 * u + w], per_lane)
                block = jnp.where(diag[w], per_lane, block)
            high, low = two_terms(block)
            at_ref[k, cr * width : (cr + 1) * width, lanes] = high
            at_ref[k, (8 + cr) * width : (9 + cr) * width, lanes] = low
        for base in (6, 14):
            at_ref[k, base * width : (base + 2) * width, lanes] = jnp.zeros((2 * width, 128), BF16)


def second_weights(taps, at_ref, k, width, keep, diag, row_is):
    for net in range(2):
        for hr in range(4):
            block = jnp.zeros((width, 128), F32)
            for w in range(3):
                per_lane = jnp.zeros((1, 128), F32)
                for u in range(3):
                    if 0 <= hr - u <= 1:
                        per_lane = jnp.where(
                            row_is[2 * net + hr - u], taps[net][3 * u + w], per_lane
                        )
                if hr in keep:
                    per_lane = per_lane * keep[hr]
                block = jnp.where(diag[w], per_lane, block)
            high, low = two_terms(block)
            rows = slice((4 * net + hr) * width, (4 * net + hr + 1) * width)
            at_ref[k, rows, 0:128] = high
            at_ref[k, rows, 128:256] = low


def minimal_filter(taps):
    parts = [[], [], [], []]
    for t in range(3):
        ends = 0.5 * (taps[t] + taps[6 + t])
        middle = 0.5 * taps[3 + t]
        for part, row in zip(parts, (taps[t], ends + middle, ends - middle, taps[6 + t])):
            part.append(row)
    return sum(parts, [])


def b_taps(load, weights, emit, width):
    top = sublane((8, 128)) == 0
    bottom = sublane((8, 128)) == 7

    def column(jb):
        even, odd = load(2 * jb), load(2 * jb + 1)
        above = jnp.where(top, 0.0, pltpu.roll(odd, 1, 0))
        below = jnp.where(bottom, 0.0, pltpu.roll(even, 7, 0))
        return above - odd, even + odd, odd - even, even - below

    window = [None, column(0), column(1)]
    for jb in range(width):
        sums = []
        for part in range(4):
            total = None
            for t in range(3):
                if window[t] is None:
                    continue
                term = weights[3 * part + t] * window[t][part]
                total = term if total is None else total + term
            sums.append(total)
        emit(jb, sums)
        yield
        window = [window[1], window[2], column(jb + 2) if jb + 2 < width else None]


def pair_of(sums):
    first, second, third, fourth = sums
    return jnp.concatenate([first + second + third, second - third - fourth], axis=0)


def prepare_kernel(width, packed_ref, at1_ref, at2_ref, w1_ref, w2_ref):
    index = lax.axis_index("arow")
    keep = {
        0: (index != 0).astype(F32),
        3: (index != lax.axis_size("arow") - 1).astype(F32),
    }

    half_lanes = lane((1, 128)) < 64
    col = lane((width, 128)) % width
    diag = [sublane((width, 128)) + 1 - col == w for w in range(3)]
    row_is = [lane((1, 128)) // width == r for r in range(4)]
    for k in range(8):
        banks = [
            [jnp.full((1, 128), packed_ref[3 * n + tap // 3, tap % 3, k], F32) for tap in range(9)]
            for n in range(4)
        ]
        first, second = banks[0:2], banks[2:4]
        first_weights(first, at1_ref, k, width, diag, row_is)
        second_weights(second, at2_ref, k, width, keep, diag, row_is)
        for net in range(2):
            for n, row in enumerate(minimal_filter(first[1 - net])):
                w1_ref[2 * k + net, n : n + 1] = row
            w1_ref[2 * k + net, 12:13] = jnp.full((1, 128), packed_ref[12, 0, k], F32)
        mixed = [jnp.where(half_lanes, second[1][tap], second[0][tap]) for tap in range(9)]
        for n, row in enumerate(minimal_filter(mixed)):
            w2_ref[k, n : n + 1] = row


def pack(bias, *banks):
    packed = jnp.pad(bias.reshape(1, 1, 8), ((12, 0), (0, 2), (0, 0)))
    for n, f in enumerate(banks):
        packed += jnp.pad(f.transpose(1, 2, 0), ((3 * n, 10 - 3 * n), (0, 0), (0, 0)))
    return packed


def prepare(packed, width):
    vmem = pl.BlockSpec(memory_space=pltpu.VMEM)
    return pl.pallas_call(
        functools.partial(prepare_kernel, width),
        out_shape=(
            jax.ShapeDtypeStruct((8, 512, 256), BF16),
            jax.ShapeDtypeStruct((8, 256, 256), BF16),
            jax.ShapeDtypeStruct((16, 16, 128), F32),
            jax.ShapeDtypeStruct((8, 16, 128), F32),
        ),
        in_specs=[pl.BlockSpec(memory_space=pltpu.SMEM)],
        out_specs=(vmem,) * 4,
        compiler_params=pltpu.CompilerParams(vmem_limit_bytes=16 << 20),
        cost_estimate=pl.CostEstimate(
            flops=2_000_000_000, bytes_accessed=3_500_000, transcendentals=0
        ),
    )(packed)


def consensus_kernel(
    offsets,
    width,
    bias2_ref,
    at1_ref,
    at2_ref,
    w1_ref,
    w2_ref,
    own_ref,
    mate_ref,
    outer_ref,
    score_ref,
    best_ref,
    fa_ref,
    vf_ref,
    vp_ref,
    s_ref,
    h_ref,
    t_ref,
    acc_ref,
    nat_ref,
):
    half = len(offsets)
    channels = own_ref.shape[2]
    index = lax.axis_index("arow")
    parity = index % 2
    inside = jnp.logical_and(index != 0, index != lax.axis_size("arow") - 1)

    fa_ref[2:4] = own_ref[half : half + 2]
    fa_ref[pl.ds(4 - 4 * parity, 2)] = mate_ref[half : half + 2]
    fa_ref[pl.ds(4 * parity, 2)] = outer_ref[...] * inside.astype(BF16)
    fa_ref[6:8] = jnp.zeros((2, width, channels), BF16)
    rows = fa_ref[...].reshape(8 * width, channels)

    for side, ref in enumerate((own_ref, mate_ref)):
        product = lax.dot_general(
            ref[0:half].reshape(half * width, channels),
            rows,
            (((1,), (1,)), ((), ())),
            preferred_element_type=F32,
        )
        for g in range(half):
            ib = index ^ (offsets[g] ^ side)
            start = (ib % 2) * 8 + ib // 2
            block = product[g * width : (g + 1) * width] * channels ** (-0.5)
            for c in range(2):
                vf_ref[c, pl.ds(start, width, stride=16), :] = block[
                    :, 128 * c : 128 * c + 128
                ]
    for c in range(4):
        vp_ref[:, 128 * c : 128 * c + 128] = vf_ref[c % 2, 0 : 2 * half * width].astype(BF16)

    def spread(k):
        s_ref[k % 2] = jnp.dot(vp_ref[...], at1_ref[k], preferred_element_type=F32)

    def hide(k):
        for net in range(2):
            weights = [w1_ref[2 * k + net, n : n + 1] for n in range(12)]
            bias = w1_ref[2 * k + net, 12:13]

            def load(r):
                return s_ref[k % 2, 8 * r : 8 * r + 8, 128 * net : 128 * net + 128]

            def emit(jb, sums):
                sums[1] = sums[1] + bias
                h_ref[k % 2, 16 * jb : 16 * jb + 16, 128 * net : 128 * net + 128] = jnp.maximum(
                    pair_of(sums).astype(BF16), 0
                )

            yield from b_taps(load, weights, emit, width)

    def gather_rows(k):
        both = jnp.dot(h_ref[k % 2], at2_ref[k], preferred_element_type=F32)
        t_ref[k % 2] = both[:, 0:128] + both[:, 128:256]

    def gather_taps(k):
        weights = [w2_ref[k, n : n + 1] for n in range(12)]

        def load(r):
            return t_ref[k % 2, 8 * r : 8 * r + 8, :]

        def emit(jb, sums):
            if k > 0:
                sums = [acc_ref[part, 8 * jb : 8 * jb + 8, :] + sums[part] for part in range(4)]
            if k < 7:
                for part in range(4):
                    acc_ref[part, 8 * jb : 8 * jb + 8, :] = sums[part]
            else:
                total = jnp.maximum(pair_of(sums) + bias2_ref[0], 0.0)
                nat_ref[pl.ds(jb, 8, stride=2 * width), :] = total[0:8]
                nat_ref[pl.ds(width + jb, 8, stride=2 * width), :] = total[8:16]

        yield from b_taps(load, weights, emit, width)

    for step in range(11):
        if step < 8:
            spread(step)
        if 2 <= step < 10:
            gather_rows(step - 2)
        ones = hide(step - 1) if 1 <= step < 9 else iter(())
        twos = gather_taps(step - 3) if step >= 3 else iter(())
        for _ in range(width):
            next(ones, None)
            next(twos, None)
            next(ones, None)

    turned = jnp.transpose(nat_ref[0 : 2 * half * width], (1, 0))
    score = turned[0:64] + turned[64:128]
    best_ref[...] = jnp.max(score, axis=0, keepdims=True)
    score_ref[...] = score


def consensus(bias_second, weights, own, mate, outer, offsets, width):
    half = len(offsets)
    cells = 2 * half * width
    channels = own.shape[2]
    vmem = pl.BlockSpec(memory_space=pltpu.VMEM)
    return pl.pallas_call(
        functools.partial(consensus_kernel, offsets, width),
        out_shape=(
            jax.ShapeDtypeStruct((2 * width, cells), F32),
            jax.ShapeDtypeStruct((1, cells), F32),
        ),
        in_specs=[pl.BlockSpec(memory_space=pltpu.SMEM)] + [vmem] * 7,
        out_specs=(vmem, vmem),
        scratch_shapes=[
            pltpu.VMEM((8, width, channels), BF16),
            pltpu.VMEM((2, cells + 16, 128), F32),
            pltpu.VMEM((cells, 512), BF16),
            pltpu.VMEM((2, cells, 256), F32),
            pltpu.VMEM((2, cells, 256), BF16),
            pltpu.VMEM((2, cells, 128), F32),
            pltpu.VMEM((4, cells // 2, 128), F32),
            pltpu.VMEM((cells + 2 * width, 128), F32),
        ],
        compiler_params=pltpu.CompilerParams(vmem_limit_bytes=32 << 20),
        cost_estimate=pl.CostEstimate(
            flops=2_000_000_000, bytes_accessed=4_500_000, transcendentals=0
        ),
    )(bias_second, *weights, own, mate, outer)


def exchange(value, mask, count):
    return lax.ppermute(value, "arow", [(i, i ^ mask) for i in range(count)])


def outer_pairs(groups, count):
    pairs = []
    for g in range(groups):
        for i in range(count):
            j = i + 1 if i % 2 else i - 1
            if 0 <= j < count:
                pairs.append((g * count + i, g * count + j))
            else:
                other = g ^ 1 if (g ^ 1) < groups else g
                pairs.append((g * count + i, other * count + i))
    return pairs


def fast(feat_a, feat_b, a_first, b_first, bias_first, a_second, b_second, bias_second):
    count = lax.axis_size("arow")
    groups = lax.axis_size("groups")
    width = feat_b.shape[1]
    masks = [(1 << b) | 1 for b in reversed(range(1, count.bit_length() - 1))]

    rows = feat_a.shape[0]
    near = lax.optimization_barrier(jnp.concatenate([feat_a, feat_b], axis=0))
    near_a, near_b = near[:rows], near[rows:]
    packed = pack(bias_first, a_first, b_first, a_second, b_second)
    held, offsets = feat_b, [0]
    for n, mask in enumerate(masks):
        if n == 1:
            feat_a, held, packed = lax.optimization_barrier((feat_a, held, packed))
            outer = lax.ppermute(feat_a, ("groups", "arow"), outer_pairs(groups, count))
        if n == 2:
            packed, held = lax.optimization_barrier((packed, held))
            weights = prepare(packed, width)
        received = exchange(held, mask, count)
        held = jnp.concatenate([near_b if n == 0 else held, received], axis=0)
        offsets = offsets + [o ^ mask for o in offsets]
    held, outer, weights, bias_second = lax.optimization_barrier(
        (held, outer, weights, bias_second)
    )
    own = jnp.concatenate([held, near_a], axis=0)
    mate = exchange(own, 1, count)

    score, best = consensus(bias_second, weights, own, mate, outer, offsets, width)
    part = lax.optimization_barrier(
        score * (score / (jnp.max(score, axis=1, keepdims=True) + EPSILON))
    )
    for mask in [1] + masks[::-1]:
        best = jnp.maximum(best, exchange(best, mask, count))
    out = part * (score / (best + EPSILON))
    return out.reshape(feat_a.shape[0], width, -1)


def on_device(feat_a, feat_b, *filters):
    count = lax.axis_size("arow")
    fits = (
        feat_a.shape == (2, 32, 256)
        and feat_b.shape == (1, 32, 256)
        and count == 16
        and filters[0].shape[0] == 8
    )
    return (fast if fits else general)(feat_a, feat_b, *filters)


def solution(mesh):
    return jax.shard_map(
        on_device,
        mesh=mesh,
        in_specs=(
            P(("groups", "arow"), None, None),
            P(("groups", "arow"), None, None),
            P(),
            P(),
            P(),
            P(),
            P(),
            P(),
        ),
        out_specs=P(("groups", "arow"), None, None),
        check_vma=False,
    )
```
